256 devices in a mesh: wide: 64 (over z, y, core), lev: 4 (over x).
Axes of the slice: x: 4, y: 4, z: 8, core: 2. Of those that a mesh axis runs over, the one named last changes fastest.
Arguments:
- spec_in: bfloat16 [320, 2, 4, 641], P('wide', None, 'lev'), may hold values from -0.0068359375 to 0.0068359375
- legendre: bfloat16 [320, 641, 1280], P('wide'), may hold values from -4 to 4
- wind: bfloat16 [1280, 4, 2560], P(('wide', 'lev')), may hold values from -6 to 6
- lat_weight: float32 [1280], replicated, may hold values from 1 to 4
- wave_order: int32 [640], replicated, may hold values from 0 to 639, as said below
- lat_order: int32 [1280], replicated, may hold values from 0 to 1279, each once
- active: int32 [1280], replicated, may hold values from 5 to 640, as said below
Outputs:
- grid: bfloat16 [1280, 4, 2560], P(('wide', 'lev'))
- spec_out: float32 [320, 2, 4, 641], P('wide', None, 'lev')
The draws below stay inside these ranges and needn't reach their ends.
Inputs may be any that keep to these rules, and one draw needn't show every extreme that they name: `wave_order`: A permutation in which slots 2p and 2p + 1 hold wavenumbers m and 639 - m. `lat_order`: each latitude once. `active`: equals 640 at some latitudes of every draw.
All inputs are finite; a program needn't handle non-finite values.
Results may differ from the reference program's by a relative error of at most 0.0072.
Values may be sent and summed in bfloat16 or wider, within the bound.
No kernel may reach another device: no remote copies, remote signals or barrier semaphores. Data moves between devices by JAX's collectives and lax.ppermute only.
A program may use at most 64 MiB of HBM per device.

```python
import math
import jax
import jax.numpy as jnp
from jax import lax

M = 640
NLAT = 1280
L = 4
PAIRS = 320
COEF = 641
PTS = 2560


def draw_wave_order(key, part):
    pair_total = M // 2
    picked = jax.random.permutation(jax.random.fold_in(key, 11), pair_total).astype(jnp.int32)
    flips = jax.random.randint(jax.random.fold_in(key, 12), (pair_total,), 0, 2).astype(jnp.int32)
    first_waves = jnp.where(flips == 1, M - 1 - picked, picked)
    second_waves = M - 1 - first_waves
    return jnp.stack([first_waves, second_waves], 1).reshape(M).astype(jnp.int32)


def draw_active(key, part):
    lat_ids = jnp.arange(NLAT, dtype=jnp.int32)
    distance = jnp.minimum(lat_ids, NLAT - 1 - lat_ids)
    jitter = jax.random.randint(jax.random.fold_in(key, 21), (NLAT,), 0, 4).astype(jnp.int32)
    return jnp.minimum(M, 5 + distance + jitter).astype(jnp.int32)


def level_of(stream_key, extent, pieces, low, high):
    gain = 1.0
    for position, parts in pieces:
        heights = jax.random.uniform(jax.random.fold_in(jax.random.fold_in(stream_key, 6), position), (parts,), jnp.float32, low / len(pieces), high / len(pieces))
        gain = gain * jnp.repeat(jnp.exp(heights), extent[position] // parts).reshape((-1,) + (1,) * (len(extent) - 1 - position))
    return gain


def noise(own_key, extent, spread, most, pieces=(), kind=jnp.bfloat16):
    array = spread * jax.random.normal(own_key, extent, jnp.float32)
    if pieces:
        array = array * level_of(own_key, extent, pieces, -0.22, 0.18)
    return jnp.clip(array, -most, most).astype(kind)


def setup_inputs(seed: int = 0) -> dict:
    seeds = jax.random.split(jax.random.key(seed), 8)
    return {
        "spec_in": noise(seeds[0], (PAIRS, 2, L, COEF), (2 * M * M) ** -0.5, 0.0068359375, ((0, 64), (2, 4))),
        "legendre": noise(seeds[1], (PAIRS, COEF, NLAT), 1.0, 4.0, ((0, 64),)),
        "wind": noise(seeds[2], (NLAT, L, PTS), 1.0, 6.0, ((0, 256),)),
        "lat_weight": jnp.clip(jnp.exp(jax.random.uniform(seeds[3], (NLAT,), jnp.float32, math.log(1.0), math.log(4.0))), 1.0, 4.0),
        "wave_order": draw_wave_order(jax.random.fold_in(seeds[7], 71), 0),
        "lat_order": jax.random.permutation(seeds[5], NLAT).astype(jnp.int32),
        "active": draw_active(jax.random.fold_in(seeds[7], 71), 0),
    }


def make_basis(wave_order, live_count, points):
    cell_count = 4 * live_count
    cell_float = cell_count.astype(jnp.float32)
    outer_count = points // 128
    outer_ids = jnp.arange(outer_count, dtype=jnp.int32) * 128
    inner_ids = jnp.arange(128, dtype=jnp.int32)
    outer_phase = (wave_order[:, None] * outer_ids[None, :]) % cell_count
    inner_phase = (wave_order[:, None] * inner_ids[None, :]) % cell_count
    outer_angle = outer_phase.astype(jnp.float32) * (2.0 * math.pi) / cell_float
    inner_angle = inner_phase.astype(jnp.float32) * (2.0 * math.pi) / cell_float
    cos_outer = jnp.cos(outer_angle)[:, :, None]
    sin_outer = jnp.sin(outer_angle)[:, :, None]
    cos_inner = jnp.cos(inner_angle)[:, None, :]
    sin_inner = jnp.sin(inner_angle)[:, None, :]
    wave_total = wave_order.shape[0]
    cosine = (cos_outer * cos_inner - sin_outer * sin_inner).reshape(wave_total, points)
    sines = (-(sin_outer * cos_inner + cos_outer * sin_inner)).reshape(wave_total, points)
    columns = jnp.arange(points, dtype=jnp.int32)
    alive = (wave_order[:, None] < live_count) & (columns[None, :] < cell_count)
    cosine = jnp.where(alive, cosine, jnp.zeros_like(cosine))
    sines = jnp.where(alive, sines, jnp.zeros_like(sines))
    return jnp.concatenate([cosine, sines], 0).astype(jnp.bfloat16)


def reference(spec_in, legendre, wind, lat_weight, wave_order, lat_order, active):
    wave_total = wave_order.shape[0]
    pair_total = wave_total // 2
    coef_count = wave_total + 1
    lat_total = legendre.shape[2]
    levels = wind.shape[1]
    points = wind.shape[2]
    first_waves = wave_order[0::2]
    owned = jnp.arange(coef_count, dtype=jnp.int32)[None, :] < (wave_total - first_waves)[:, None]

    def inverse_pair(inputs):
        leg_block, row_mask, spec_rows = inputs
        nothing = jnp.zeros_like(spec_rows)
        stacked = jnp.stack([jnp.where(row_mask, spec_rows, nothing), jnp.where(row_mask, nothing, spec_rows)], 0)
        result = jnp.einsum('srlc,cq->srlq', stacked.astype(jnp.float32), leg_block.astype(jnp.float32))
        return result.astype(jnp.bfloat16)

    fourier = lax.map(inverse_pair, (legendre, owned, spec_in))
    fourier = fourier.reshape(wave_total, 2, levels, lat_total)
    by_lat = jnp.transpose(fourier, (3, 2, 1, 0))
    factors = jnp.where(wave_order == 0, 1.0, 2.0).astype(jnp.bfloat16)

    def per_lat(inputs):
        coeffs, wind_rows, live_count, weight = inputs
        basis_rows = make_basis(wave_order, live_count, points)
        scaled = (coeffs * factors).reshape(levels, 2 * wave_total)
        grid_rows = jnp.dot(scaled, basis_rows, preferred_element_type=jnp.float32).astype(jnp.bfloat16)
        product = (grid_rows.astype(jnp.float32) * wind_rows.astype(jnp.float32)).astype(jnp.bfloat16)
        folded = lax.dot_general(product, basis_rows, (((1,), (1,)), ((), ())), preferred_element_type=jnp.float32)
        folded = (folded * (weight / (4 * live_count).astype(jnp.float32))).astype(jnp.bfloat16)
        return grid_rows, folded.reshape(levels, 2, wave_total)

    grid, folded = lax.map(per_lat, (by_lat[lat_order], wind, active[lat_order], lat_weight[lat_order]))
    back_geo = jnp.zeros_like(folded).at[lat_order].set(folded)
    per_pair = jnp.transpose(back_geo.reshape(lat_total, levels, 2, pair_total, 2), (3, 4, 2, 1, 0))

    def direct_pair(inputs):
        leg_block, row_mask, lat_rows = inputs
        results = jnp.einsum('srlq,cq->srlc', lat_rows.astype(jnp.float32), leg_block.astype(jnp.float32))
        return jnp.where(row_mask, results[0], results[1])

    spec_out = lax.map(direct_pair, (legendre, owned, per_pair))
    return grid, spec_out
```

```python
import math

import jax
import jax.numpy as jnp
from jax import lax
from jax.experimental import pallas as pl
from jax.experimental.pallas import tpu as pltpu
from jax.sharding import PartitionSpec as P

F32 = jnp.float32
BF16 = jnp.bfloat16
I32 = jnp.int32
NT = (((1,), (1,)), ((), ()))


def iota(shape, axis):
    return lax.broadcasted_iota(I32, shape, axis)


def pick(table_ref, first_row, row_count, index):
    row = index >> 7
    lane = index & 127
    out = jnp.zeros(index.shape, I32)
    for k in range(row_count):
        line = jnp.broadcast_to(table_ref[first_row + k : first_row + k + 1, :], index.shape)
        got = jnp.take_along_axis(line, lane, axis=1, mode="promise_in_bounds")
        out = jnp.where(row == k, got, out)
    return out


def latitude_table(lat_ref, lat_here):
    halves = []
    index = iota((8, 128), 1) * lat_here + jnp.minimum(iota((8, 128), 0), lat_here - 1)
    for h in range(2):
        halves.append(pick(lat_ref, h * lat_here, lat_here, index))
    return jnp.concatenate(halves, 1)


def fill_onehot(onehot_ref, lat_ref, lat_here):
    lat_total = onehot_ref.shape[0]
    table = latitude_table(lat_ref, lat_here)
    for i in range(lat_here):
        for block in range(0, lat_total, 256):
            rows = iota((256, 256), 0) + block
            hit = rows == table[i : i + 1, :]
            onehot_ref[block : block + 256, i * 256 : (i + 1) * 256] = jnp.where(
                hit, 1.0, 0.0
            ).astype(BF16)


def load_legendre(leg_hbm, leg, sems):
    copies = [
        pltpu.make_async_copy(leg_hbm.at[p], leg.at[p], sems.at[p]) for p in range(leg.shape[0])
    ]
    for copy in copies:
        copy.start()
    return copies


def inverse_kernel(wave_ref, spec_ref, lat_ref, leg_hbm, out_ref, leg, onehot, four, stack, sems):
    pairs, coef, lat_total = leg.shape
    lat_here = lat_ref.shape[0] * 128 // 256
    copies = load_legendre(leg_hbm, leg, sems)
    fill_onehot(onehot, lat_ref, lat_here)
    stack[...] = jnp.zeros_like(stack)
    four[...] = jnp.zeros_like(four)
    wide = lax.axis_index("wide")
    column = iota((2, coef), 1)
    for p in range(pairs):
        first = wave_ref[wide * 2 * pairs + 2 * p]
        own = column < coef - 1 - first
        rows = spec_ref[p].astype(F32)
        nothing = jnp.zeros_like(rows)
        left = jnp.concatenate(
            [
                jnp.where(own, rows, nothing),
                jnp.where(own, nothing, rows),
                nothing,
                nothing,
            ],
            0,
        ).astype(BF16)
        copies[p].wait()
        result = jnp.dot(left, leg[p], preferred_element_type=F32)
        for s in range(2):
            for r in range(2):
                row = s * 12 + r * pairs + p
                four[row : row + 1, :] = result[2 * s + r : 2 * s + r + 1, :]
    placed = jnp.dot(four[...].astype(BF16), onehot[...], preferred_element_type=F32)
    for i in range(lat_here):
        for s in range(2):
            stack[s * 64 + i * 12 : s * 64 + i * 12 + 12, :] = placed[
                s * 12 : s * 12 + 12, i * 256 : (i + 1) * 256
            ]
    out_ref[...] = stack[...].T


def direct_kernel(wave_ref, recv_ref, lat_ref, leg_hbm, out_ref, leg, onehot, sems):
    pairs, coef, lat_total = leg.shape
    lat_here = lat_ref.shape[0] * 128 // 256
    copies = load_legendre(leg_hbm, leg, sems)
    fill_onehot(onehot, lat_ref, lat_here)
    wide = lax.axis_index("wide")
    turned = recv_ref[...].T
    pieces = []
    for i in range(lat_here):
        pieces.append(
            jnp.concatenate(
                [turned[i * 12 : i * 12 + 12, :], turned[64 + i * 12 : 64 + i * 12 + 12, :]], 0
            )
        )
    slots = jnp.concatenate(pieces, 1).astype(BF16)
    ordered = lax.dot_general(slots, onehot[...], NT, preferred_element_type=F32)
    column = iota((1, coef), 1)
    for p in range(pairs):
        first = wave_ref[wide * 2 * pairs + 2 * p]
        own = column < coef - 1 - first
        left = jnp.concatenate(
            [
                ordered[s * 12 + r * pairs + p : s * 12 + r * pairs + p + 1, :]
                for s in range(2)
                for r in range(2)
            ]
            + [jnp.zeros((4, lat_total), F32)],
            0,
        ).astype(BF16)
        copies[p].wait()
        result = lax.dot_general(left, leg[p], NT, preferred_element_type=F32)
        for r in range(2):
            out_ref[p, r, :, :] = jnp.where(own, result[r : r + 1, :], result[2 + r : 3 + r, :])


def turn(x):
    half = x * math.pi
    sq = half * half
    sine = -1.0 / 39916800
    for c in (1.0 / 362880, -1.0 / 5040, 1.0 / 120, -1.0 / 6, 1.0):
        sine = sine * sq + c
    sine = sine * half
    cosine = 1.0 / 479001600
    for c in (-1.0 / 3628800, 1.0 / 40320, -1.0 / 720, 1.0 / 24, -0.5, 1.0):
        cosine = cosine * sq + c
    return 1.0 - 2.0 * sine * sine, 2.0 * sine * cosine


def fill_perm(perm):
    for block in range(0, 512, 256):
        row = iota((256, 512), 0)
        target = (row & 3) * 128 + (block // 256) * 64 + (row >> 2)
        hit = target == iota((256, 512), 1)
        perm[block : block + 256, :] = jnp.where(hit, 1.0, 0.0).astype(BF16)


def fourier_kernel(
    lato_ref, active_ref, weight_ref, recv_ref, wave_ref, wind_ref,
    grid_ref, out_ref,
    perm, four, table, left, backs,
):
    lat_here, levels, points = wind_ref.shape
    blocks = wave_ref.shape[0]
    half = blocks * 128
    outer = points // 128
    fill_perm(perm)
    turned = recv_ref[...].T.astype(BF16)
    joined = jnp.concatenate([turned[:64, :], turned[64:, :]], 1)
    spread = jnp.dot(joined, perm[...], preferred_element_type=F32)
    for l in range(4):
        for copy in range(2):
            four[pl.ds(copy * 4 + l, 64, stride=8), :] = spread[:, l * 128 : (l + 1) * 128]
    backs[...] = jnp.zeros_like(backs)

    lane = iota((8, 128), 1)
    row = iota((8, 128), 0)
    index = (lane & 63) * (2 * blocks) + 2 * jnp.minimum(row, blocks - 1) + (lane >> 6)
    waves = pick(wave_ref, 0, blocks, index)
    waves_f = waves.astype(F32)
    steps_low = row.astype(F32)
    steps_high = jnp.where(row == 0, 8.0, jnp.where(row == 1, 128.0, 256.0))
    upper = row < 4
    first_slot = (lax.axis_index("wide") * lax.axis_size("lev") + lax.axis_index("lev")) * lat_here
    outer_row = iota((outer * 4, 128), 0) >> 2
    point = outer_row * 128 + iota((outer * 4, 128), 1)

    for i in range(lat_here):
        lat = lato_ref[first_slot + i]
        live = jnp.full((8, 128), active_ref[lat], I32)
        cells = (live * 4).astype(F32)
        inverse = 1.0 / cells
        gain = jnp.full((8, 128), weight_ref[lat], F32) / cells
        keep = []
        for p in range(blocks):
            wave = jnp.broadcast_to(waves_f[p : p + 1, :], (8, 128))
            alive = jnp.broadcast_to(waves[p : p + 1, :], (8, 128)) < live
            angles = []
            for steps in (steps_low, steps_high):
                phase = wave * steps
                rest = phase - jnp.round(phase * inverse) * cells
                angles.append(turn(rest * inverse))
            (cos_b, sin_b), (cos_h, sin_h) = angles
            cos8 = jnp.broadcast_to(cos_h[0:1, :], (8, 128))
            sin8 = jnp.broadcast_to(sin_h[0:1, :], (8, 128))
            cosx = jnp.where(upper, 1.0, jnp.broadcast_to(cos_h[1:2, :], (8, 128)))
            sinx = jnp.where(upper, 0.0, jnp.broadcast_to(sin_h[1:2, :], (8, 128)))
            cos2 = jnp.broadcast_to(cos_h[2:3, :], (8, 128))
            sin2 = jnp.broadcast_to(sin_h[2:3, :], (8, 128))
            keep.append((cosx, sinx, cos2, sin2, alive))
            lo, hi = p * 128, half + p * 128
            held = []
            for b in range(16):
                held.append((cos_b, sin_b))
                if b % 2:
                    at = (b - 1) * 8
                    table[at : at + 16, lo : lo + 128] = jnp.concatenate(
                        [held[b - 1][0], cos_b], 0
                    ).astype(BF16)
                    table[at : at + 16, hi : hi + 128] = jnp.concatenate(
                        [held[b - 1][1], sin_b], 0
                    ).astype(BF16)
                if b < 15:
                    cos_b, sin_b = cos_b * cos8 - sin_b * sin8, sin_b * cos8 + cos_b * sin8
            at = (i * 12 + p) * 8
            real = four[at : at + 8, :]
            at = (i * 12 + blocks + p) * 8
            imag = four[at : at + 8, :]
            scale = jnp.where(alive, jnp.where(wave == 0.0, 1.0, 2.0), 0.0)
            real = real * scale
            imag = imag * scale
            real, imag = real * cosx - imag * sinx, real * sinx + imag * cosx
            held = []
            for a in range(outer // 2):
                held.append((real, imag))
                if a % 2:
                    at = (a - 1) * 8
                    left[at : at + 16, lo : lo + 128] = jnp.concatenate(
                        [held[a - 1][0], real], 0
                    ).astype(BF16)
                    left[at : at + 16, hi : hi + 128] = -jnp.concatenate(
                        [held[a - 1][1], imag], 0
                    ).astype(BF16)
                if a < outer // 2 - 1:
                    real, imag = real * cos2 - imag * sin2, real * sin2 + imag * cos2
        values = lax.dot_general(left[...], table[...], NT, preferred_element_type=F32)
        inside = point < active_ref[lat] * 4
        values = jnp.where(inside, values, 0.0).astype(BF16).astype(F32)
        winds = []
        for a in range(outer):
            grid_ref[i, :, a * 128 : (a + 1) * 128] = values[a * 4 : a * 4 + 4, :].astype(BF16)
            winds.append(wind_ref[i, :, a * 128 : (a + 1) * 128].astype(F32))
        product = (values * jnp.concatenate(winds, 0)).astype(BF16)
        sums = jnp.dot(product, table[...], preferred_element_type=F32)
        for p in range(blocks):
            cosx, sinx, cos2, sin2, alive = keep[p]
            lo, hi = p * 128, half + p * 128
            last = outer * 4 - 8
            real = sums[last : last + 8, lo : lo + 128]
            imag = sums[last : last + 8, hi : hi + 128]
            for at in range(last - 8, -1, -8):
                real, imag = (
                    sums[at : at + 8, lo : lo + 128] + (real * cos2 - imag * sin2),
                    sums[at : at + 8, hi : hi + 128] + (real * sin2 + imag * cos2),
                )
            real, imag = real * cosx - imag * sinx, real * sinx + imag * cosx
            real = real + pltpu.roll(real, 4, 0)
            imag = imag + pltpu.roll(imag, 4, 0)
            both = jnp.where(alive, jnp.where(upper, real, -imag) * gain, 0.0)
            at = (i * 12 + p) * 4
            backs[at : at + 4, :] = both[0:4, :]
            at = (i * 12 + blocks + p) * 4
            backs[at : at + 4, :] = both[4:8, :]

    joined = jnp.concatenate([backs[pl.ds(l, 64, stride=4), :] for l in range(4)], 1)
    spread = lax.dot_general(joined.astype(BF16), perm[...], NT, preferred_element_type=F32)
    out_ref[...] = jnp.concatenate([spread[:, :256], spread[:, 256:]], 0).T


def vmem():
    return pl.BlockSpec(memory_space=pltpu.VMEM)


def smem():
    return pl.BlockSpec(memory_space=pltpu.SMEM)


def exchange(rows):
    count, width = rows.shape
    moved = lax.all_to_all(
        rows.reshape(count, 1, width), ("wide", "lev"), split_axis=0, concat_axis=0, tiled=True
    )
    return moved.reshape(count, width)


def shards(spec_in, legendre, wind, lat_weight, wave_order, lat_order, active):
    pairs, coef, lat_total = legendre.shape
    lat_here, levels, points = wind.shape
    devices = lax.axis_size("wide") * lax.axis_size("lev")
    limit = pltpu.CompilerParams(vmem_limit_bytes=40 * 1024 * 1024)
    lat_rows = lat_order.reshape(lat_total // 128, 128)
    wave_rows = wave_order.reshape(wave_order.shape[0] // 128, 128)
    any_space = pl.BlockSpec(memory_space=pl.ANY)

    outgoing = pl.pallas_call(
        inverse_kernel,
        name="legendre_inverse",
        out_shape=jax.ShapeDtypeStruct((devices, 128), F32),
        in_specs=[smem(), vmem(), vmem(), any_space],
        out_specs=vmem(),
        scratch_shapes=[
            pltpu.VMEM((pairs, coef, lat_total), BF16),
            pltpu.VMEM((lat_total, lat_here * devices), BF16),
            pltpu.VMEM((24, lat_total), F32),
            pltpu.VMEM((128, devices), F32),
            pltpu.SemaphoreType.DMA((pairs,)),
        ],
        compiler_params=limit,
    )(wave_order, spec_in.reshape(pairs, 2, coef), lat_rows, legendre)

    grid, outgoing = pl.pallas_call(
        fourier_kernel,
        name="fourier",
        out_shape=(
            jax.ShapeDtypeStruct(wind.shape, BF16),
            jax.ShapeDtypeStruct((devices, 128), F32),
        ),
        in_specs=[smem(), smem(), smem(), vmem(), vmem(), vmem()],
        out_specs=(vmem(), vmem()),
        scratch_shapes=[
            pltpu.VMEM((512, 512), BF16),
            pltpu.VMEM((512, 128), F32),
            pltpu.VMEM((128, 2 * wave_order.shape[0]), BF16),
            pltpu.VMEM((points // 32, 2 * wave_order.shape[0]), BF16),
            pltpu.VMEM((256, 128), F32),
        ],
        compiler_params=limit,
    )(lat_order, active, lat_weight, exchange(outgoing), wave_rows, wind)

    spec_out = pl.pallas_call(
        direct_kernel,
        name="legendre_direct",
        out_shape=jax.ShapeDtypeStruct((pairs, 2, 1, coef), F32),
        in_specs=[smem(), vmem(), vmem(), any_space],
        out_specs=vmem(),
        scratch_shapes=[
            pltpu.VMEM((pairs, coef, lat_total), BF16),
            pltpu.VMEM((lat_total, lat_here * devices), BF16),
            pltpu.SemaphoreType.DMA((pairs,)),
        ],
        compiler_params=limit,
    )(wave_order, exchange(outgoing), lat_rows, legendre)
    return (grid, spec_out)


def solution(mesh):
    in_specs = (
        P("wide", None, "lev", None),
        P("wide", None, None),
        P(("wide", "lev"), None, None),
        P(),
        P(),
        P(),
        P(),
    )
    out_specs = (P(("wide", "lev"), None, None), P("wide", None, "lev", None))
    return jax.shard_map(shards, mesh=mesh, in_specs=in_specs, out_specs=out_specs, check_vma=False)
```

```python
import math

import jax
import jax.numpy as jnp
from jax import lax
from jax.experimental import pallas as pl
from jax.experimental.pallas import tpu as pltpu
from jax.sharding import PartitionSpec as P

F32 = jnp.float32
BF16 = jnp.bfloat16
I32 = jnp.int32
NT = (((1,), (1,)), ((), ()))


def iota(shape, axis):
    return lax.broadcasted_iota(I32, shape, axis)


def pick(table_ref, first_row, row_count, index):
    row = index >> 7
    lane = index & 127
    out = jnp.zeros(index.shape, I32)
    for k in range(row_count):
        line = jnp.broadcast_to(table_ref[first_row + k : first_row + k + 1, :], index.shape)
        got = jnp.take_along_axis(line, lane, axis=1, mode="promise_in_bounds")
        out = jnp.where(row == k, got, out)
    return out


def latitude_table(lat_ref, lat_here):
    halves = []
    index = iota((8, 128), 1) * lat_here + jnp.minimum(iota((8, 128), 0), lat_here - 1)
    for h in range(2):
        halves.append(pick(lat_ref, h * lat_here, lat_here, index))
    return jnp.concatenate(halves, 1)


def fill_onehot(onehot_ref, lat_ref, lat_here):
    lat_total = onehot_ref.shape[0]
    table = latitude_table(lat_ref, lat_here)
    for i in range(lat_here):
        for block in range(0, lat_total, 256):
            rows = iota((256, 256), 0) + block
            hit = rows == table[i : i + 1, :]
            onehot_ref[block : block + 256, i * 256 : (i + 1) * 256] = jnp.where(
                hit, 1.0, 0.0
            ).astype(BF16)


def turn(x):
    half = x * math.pi
    sq = half * half
    sine = -1.0 / 39916800
    for c in (1.0 / 362880, -1.0 / 5040, 1.0 / 120, -1.0 / 6, 1.0):
        sine = sine * sq + c
    sine = sine * half
    cosine = 1.0 / 479001600
    for c in (-1.0 / 3628800, 1.0 / 40320, -1.0 / 720, 1.0 / 24, -0.5, 1.0):
        cosine = cosine * sq + c
    return 1.0 - 2.0 * sine * sine, 2.0 * sine * cosine


def fill_perm(perm):
    for block in range(0, 512, 256):
        row = iota((256, 512), 0)
        target = (row & 3) * 128 + (block // 256) * 64 + (row >> 2)
        hit = target == iota((256, 512), 1)
        perm[block : block + 256, :] = jnp.where(hit, 1.0, 0.0).astype(BF16)


def wave_table(wave_rows_ref, blocks):
    lane = iota((8, 128), 1)
    row = iota((8, 128), 0)
    index = (lane & 63) * (2 * blocks) + 2 * jnp.minimum(row, blocks - 1) + (lane >> 6)
    return pick(wave_rows_ref, 0, blocks, index)


def fill_tables(table, rotors, wave_rows_ref, lato_ref, active_ref, weight_ref):
    lat_here = table.shape[0]
    blocks = wave_rows_ref.shape[0]
    half = blocks * 128
    row = iota((8, 128), 0)
    waves = wave_table(wave_rows_ref, blocks)
    waves_f = waves.astype(F32)
    steps_low = row.astype(F32)
    steps_high = jnp.where(row == 0, 8.0, jnp.where(row == 1, 128.0, 256.0))
    first_slot = (lax.axis_index("wide") * lax.axis_size("lev") + lax.axis_index("lev")) * lat_here
    for i in range(lat_here):
        lat = lato_ref[first_slot + i]
        live = jnp.full((8, 128), active_ref[lat], I32)
        cells = (live * 4).astype(F32)
        inverse = 1.0 / cells
        gain = jnp.full((8, 128), weight_ref[lat], F32) / cells
        for p in range(blocks):
            wave = jnp.broadcast_to(waves_f[p : p + 1, :], (8, 128))
            alive = jnp.broadcast_to(waves[p : p + 1, :], (8, 128)) < live
            angles = []
            for steps in (steps_low, steps_high):
                phase = wave * steps
                rest = phase - jnp.round(phase * inverse) * cells
                angles.append(turn(rest * inverse))
            (cos_b, sin_b), (cos_h, sin_h) = angles
            cos8 = jnp.broadcast_to(cos_h[0:1, :], (8, 128))
            sin8 = jnp.broadcast_to(sin_h[0:1, :], (8, 128))
            lo, hi = p * 128, half + p * 128
            held = []
            for b in range(16):
                held.append((cos_b, sin_b))
                if b % 2:
                    at = (b - 1) * 8
                    table[i, at : at + 16, lo : lo + 128] = jnp.concatenate(
                        [held[b - 1][0], cos_b], 0
                    ).astype(BF16)
                    table[i, at : at + 16, hi : hi + 128] = jnp.concatenate(
                        [held[b - 1][1], sin_b], 0
                    ).astype(BF16)
                if b < 15:
                    cos_b, sin_b = cos_b * cos8 - sin_b * sin8, sin_b * cos8 + cos_b * sin8
            scale = jnp.where(alive, jnp.where(wave == 0.0, 1.0, 2.0), 0.0)
            lines = (
                cos_h[1:2, :], sin_h[1:2, :], cos_h[2:3, :], sin_h[2:3, :],
                scale[0:1, :], jnp.where(alive, gain, 0.0)[0:1, :], cells[0:1, :],
            )
            at = (i * blocks + p) * 8
            for n, line in enumerate(lines):
                rotors[at + n : at + n + 1, :] = line


def inverse_kernel(
    wave_hbm, wave_rows_hbm, spec_hbm, lat_hbm, lat_rows_hbm, active_hbm, weight_hbm, leg_hbm,
    out_ref, leg, onehot, table, rotors, perm,
    wave_ref, wave_rows_ref, spec_ref, lat_ref, lat_rows_ref, active_ref, weight_ref,
    four, stack, small_sems, sems,
):
    pairs, coef, lat_total = leg.shape
    lat_here = table.shape[0]
    small = [
        pltpu.make_async_copy(source, target, small_sems.at[n])
        for n, (source, target) in enumerate(
            (
                (lat_rows_hbm, lat_rows_ref),
                (wave_rows_hbm, wave_rows_ref),
                (lat_hbm, lat_ref),
                (active_hbm, active_ref),
                (weight_hbm, weight_ref),
                (wave_hbm, wave_ref),
                (spec_hbm, spec_ref),
            )
        )
    ]
    copies = [pltpu.make_async_copy(leg_hbm.at[p], leg.at[p], sems.at[p]) for p in range(pairs)]
    for copy in small + copies:
        copy.start()
    stack[...] = jnp.zeros_like(stack)
    four[...] = jnp.zeros_like(four)
    for copy in small:
        copy.wait()
    fill_onehot(onehot, lat_rows_ref, lat_here)
    fill_tables(table, rotors, wave_rows_ref, lat_ref, active_ref, weight_ref)
    fill_perm(perm)
    wide = lax.axis_index("wide")
    column = iota((2, coef), 1)
    for p in range(pairs):
        first = wave_ref[wide * 2 * pairs + 2 * p]
        own = column < coef - 1 - first
        rows = spec_ref[p].astype(F32)
        nothing = jnp.zeros_like(rows)
        left = jnp.concatenate(
            [
                jnp.where(own, rows, nothing),
                jnp.where(own, nothing, rows),
                nothing,
                nothing,
            ],
            0,
        ).astype(BF16)
        copies[p].wait()
        result = jnp.dot(left, leg[p], preferred_element_type=F32)
        for s in range(2):
            for r in range(2):
                row = s * 12 + r * pairs + p
                four[row : row + 1, :] = result[2 * s + r : 2 * s + r + 1, :]
    placed = jnp.dot(four[...].astype(BF16), onehot[...], preferred_element_type=F32)
    for i in range(lat_here):
        for s in range(2):
            stack[s * 64 + i * 12 : s * 64 + i * 12 + 12, :] = placed[
                s * 12 : s * 12 + 12, i * 256 : (i + 1) * 256
            ]
    out_ref[...] = stack[...].T


def direct_kernel(wave_ref, recv_ref, onehot, leg, out_ref):
    pairs, coef, lat_total = leg.shape
    lat_here = lat_total // 256
    wide = lax.axis_index("wide")
    turned = recv_ref[...].T
    pieces = []
    for i in range(lat_here):
        pieces.append(
            jnp.concatenate(
                [turned[i * 12 : i * 12 + 12, :], turned[64 + i * 12 : 64 + i * 12 + 12, :]], 0
            )
        )
    slots = jnp.concatenate(pieces, 1).astype(BF16)
    ordered = lax.dot_general(slots, onehot[...], NT, preferred_element_type=F32)
    column = iota((1, coef), 1)
    for p in range(pairs):
        first = wave_ref[wide * 2 * pairs + 2 * p]
        own = column < coef - 1 - first
        left = jnp.concatenate(
            [
                ordered[s * 12 + r * pairs + p : s * 12 + r * pairs + p + 1, :]
                for s in range(2)
                for r in range(2)
            ]
            + [jnp.zeros((4, lat_total), F32)],
            0,
        ).astype(BF16)
        result = lax.dot_general(left, leg[p], NT, preferred_element_type=F32)
        for r in range(2):
            out_ref[p, r, :, :] = jnp.where(own, result[r : r + 1, :], result[2 + r : 3 + r, :])


def fourier_kernel(
    recv_ref, table, rotors, perm, wind_ref, grid_ref, out_ref, four, left, backs,
):
    lat_here, levels, points = wind_ref.shape
    half = table.shape[2] // 2
    blocks = half // 128
    outer = points // 128
    turned = recv_ref[...].T.astype(BF16)
    joined = jnp.concatenate([turned[:64, :], turned[64:, :]], 1)
    spread = jnp.dot(joined, perm[...], preferred_element_type=F32)
    for l in range(4):
        for copy in range(2):
            four[pl.ds(copy * 4 + l, 64, stride=8), :] = spread[:, l * 128 : (l + 1) * 128]
    backs[...] = jnp.zeros_like(backs)
    upper = iota((8, 128), 0) < 4
    outer_row = iota((outer * 4, 128), 0) >> 2
    point = (outer_row * 128 + iota((outer * 4, 128), 1)).astype(F32)

    def rotor(i, p, n):
        at = (i * blocks + p) * 8 + n
        return jnp.broadcast_to(rotors[at : at + 1, :], (8, 128))

    for i in range(lat_here):
        for p in range(blocks):
            cosx = jnp.where(upper, 1.0, rotor(i, p, 0))
            sinx = jnp.where(upper, 0.0, rotor(i, p, 1))
            cos2, sin2, scale = (rotor(i, p, n) for n in (2, 3, 4))
            lo, hi = p * 128, half + p * 128
            at = (i * 12 + p) * 8
            real = four[at : at + 8, :] * scale
            at = (i * 12 + blocks + p) * 8
            imag = four[at : at + 8, :] * scale
            real, imag = real * cosx - imag * sinx, real * sinx + imag * cosx
            held = []
            for a in range(outer // 2):
                held.append((real, imag))
                if a % 2:
                    at = (a - 1) * 8
                    left[i, at : at + 16, lo : lo + 128] = jnp.concatenate(
                        [held[a - 1][0], real], 0
                    ).astype(BF16)
                    left[i, at : at + 16, hi : hi + 128] = -jnp.concatenate(
                        [held[a - 1][1], imag], 0
                    ).astype(BF16)
                if a < outer // 2 - 1:
                    real, imag = real * cos2 - imag * sin2, real * sin2 + imag * cos2
        values = lax.dot_general(left[i], table[i], NT, preferred_element_type=F32)
        cells = jnp.broadcast_to(rotors[i * blocks * 8 + 6 : i * blocks * 8 + 7, :], point.shape)
        values = jnp.where(point < cells, values, 0.0).astype(BF16).astype(F32)
        winds = []
        for a in range(outer):
            grid_ref[i, :, a * 128 : (a + 1) * 128] = values[a * 4 : a * 4 + 4, :].astype(BF16)
            winds.append(wind_ref[i, :, a * 128 : (a + 1) * 128].astype(F32))
        product = (values * jnp.concatenate(winds, 0)).astype(BF16)
        sums = jnp.dot(product, table[i], preferred_element_type=F32)
        for p in range(blocks):
            cosx = jnp.where(upper, 1.0, rotor(i, p, 0))
            sinx = jnp.where(upper, 0.0, rotor(i, p, 1))
            cos2, sin2, gain = (rotor(i, p, n) for n in (2, 3, 5))
            lo, hi = p * 128, half + p * 128
            last = outer * 4 - 8
            real = sums[last : last + 8, lo : lo + 128]
            imag = sums[last : last + 8, hi : hi + 128]
            for at in range(last - 8, -1, -8):
                real, imag = (
                    sums[at : at + 8, lo : lo + 128] + (real * cos2 - imag * sin2),
                    sums[at : at + 8, hi : hi + 128] + (real * sin2 + imag * cos2),
                )
            real, imag = real * cosx - imag * sinx, real * sinx + imag * cosx
            real = real + pltpu.roll(real, 4, 0)
            imag = imag + pltpu.roll(imag, 4, 0)
            both = jnp.where(upper, real, -imag) * gain
            at = (i * 12 + p) * 4
            backs[at : at + 4, :] = both[0:4, :]
            at = (i * 12 + blocks + p) * 4
            backs[at : at + 4, :] = both[4:8, :]

    joined = jnp.concatenate([backs[pl.ds(l, 64, stride=4), :] for l in range(4)], 1)
    spread = lax.dot_general(joined.astype(BF16), perm[...], NT, preferred_element_type=F32)
    out_ref[...] = jnp.concatenate([spread[:, :256], spread[:, 256:]], 0).T


def vmem():
    return pl.BlockSpec(memory_space=pltpu.VMEM)


def hbm():
    return pl.BlockSpec(memory_space=pltpu.HBM)


def smem():
    return pl.BlockSpec(memory_space=pltpu.SMEM)


def in_hbm(x):
    return pltpu.with_memory_space_constraint(x, pltpu.HBM)


def exchange(rows):
    count, width = rows.shape
    moved = lax.all_to_all(
        rows.reshape(count, 1, width), ("wide", "lev"), split_axis=0, concat_axis=0, tiled=True
    )
    return moved.reshape(count, width)


def shards(spec_in, legendre, wind, lat_weight, wave_order, lat_order, active):
    pairs, coef, lat_total = legendre.shape
    lat_here, levels, points = wind.shape
    devices = lat_total // lat_here
    limit = pltpu.CompilerParams(vmem_limit_bytes=24 * 1024 * 1024)
    lat_rows = lat_order.reshape(lat_total // 128, 128)
    wave_rows = wave_order.reshape(wave_order.shape[0] // 128, 128)

    waves = wave_order.shape[0]
    operands = (
        wave_order, wave_rows, spec_in.reshape(pairs, 2, coef), lat_order, lat_rows, active,
        lat_weight, legendre,
    )
    outgoing, leg_here, onehot, table, rotors, perm = pl.pallas_call(
        inverse_kernel,
        name="legendre_inverse",
        out_shape=(
            jax.ShapeDtypeStruct((devices, 128), F32),
            jax.ShapeDtypeStruct(legendre.shape, BF16),
            jax.ShapeDtypeStruct((lat_total, lat_total), BF16),
            jax.ShapeDtypeStruct((lat_here, 128, 2 * waves), BF16),
            jax.ShapeDtypeStruct((lat_here * waves // 128 * 8, 128), F32),
            jax.ShapeDtypeStruct((512, 512), BF16),
        ),
        in_specs=[hbm()] * len(operands),
        out_specs=(vmem(),) * 6,
        scratch_shapes=[
            pltpu.SMEM(wave_order.shape, I32),
            pltpu.VMEM(wave_rows.shape, I32),
            pltpu.VMEM((pairs, 2, coef), BF16),
            pltpu.SMEM(lat_order.shape, I32),
            pltpu.VMEM(lat_rows.shape, I32),
            pltpu.SMEM(active.shape, I32),
            pltpu.SMEM(lat_weight.shape, F32),
            pltpu.VMEM((24, lat_total), F32),
            pltpu.VMEM((128, devices), F32),
            pltpu.SemaphoreType.DMA((7,)),
            pltpu.SemaphoreType.DMA((pairs,)),
        ],
        compiler_params=limit,
    )(*(in_hbm(x) for x in operands))

    grid, outgoing = pl.pallas_call(
        fourier_kernel,
        name="fourier",
        out_shape=(
            jax.ShapeDtypeStruct(wind.shape, BF16),
            jax.ShapeDtypeStruct((devices, 128), F32),
        ),
        in_specs=[vmem()] * 5,
        out_specs=(vmem(), vmem()),
        scratch_shapes=[
            pltpu.VMEM((512, 128), F32),
            pltpu.VMEM((lat_here, points // 32, 2 * waves), BF16),
            pltpu.VMEM((256, 128), F32),
        ],
        compiler_params=limit,
    )(exchange(outgoing), table, rotors, perm, wind)

    spec_out = pl.pallas_call(
        direct_kernel,
        name="legendre_direct",
        out_shape=jax.ShapeDtypeStruct((pairs, 2, 1, coef), F32),
        in_specs=[smem(), vmem(), vmem(), vmem()],
        out_specs=vmem(),
        compiler_params=limit,
    )(wave_order, exchange(outgoing), onehot, leg_here)
    return (grid, spec_out)


def solution(mesh):
    in_specs = (
        P("wide", None, "lev", None),
        P("wide", None, None),
        P(("wide", "lev"), None, None),
        P(),
        P(),
        P(),
        P(),
    )
    out_specs = (P(("wide", "lev"), None, None), P("wide", None, "lev", None))
    return jax.shard_map(shards, mesh=mesh, in_specs=in_specs, out_specs=out_specs, check_vma=False)
```

```python
import math

import jax
import jax.numpy as jnp
from jax import lax
from jax.experimental import pallas as pl
from jax.experimental.pallas import tpu as pltpu
from jax.sharding import PartitionSpec as P

F32 = jnp.float32
BF16 = jnp.bfloat16
I32 = jnp.int32
NT = (((1,), (1,)), ((), ()))
BUSY = pl.CostEstimate(flops=4_000_000_000, bytes_accessed=16_000_000, transcendentals=0)


def iota(shape, axis):
    return lax.broadcasted_iota(I32, shape, axis)


def pick(table_ref, first_row, row_count, index):
    row = index >> 7
    lane = index & 127
    out = jnp.zeros(index.shape, I32)
    for k in range(row_count):
        line = jnp.broadcast_to(table_ref[first_row + k : first_row + k + 1, :], index.shape)
        got = jnp.take_along_axis(line, lane, axis=1, mode="promise_in_bounds")
        out = jnp.where(row == k, got, out)
    return out


def latitude_table(lat_ref, lat_here):
    halves = []
    index = iota((8, 128), 1) * lat_here + jnp.minimum(iota((8, 128), 0), lat_here - 1)
    for h in range(2):
        halves.append(pick(lat_ref, h * lat_here, lat_here, index))
    return jnp.concatenate(halves, 1)


def gather_tiles(tiles, index):
    tile = index >> 7
    lane = index & 127
    out = jnp.zeros(index.shape, tiles[0].dtype)
    for k, source in enumerate(tiles):
        got = jnp.take_along_axis(source, lane, axis=1, mode="promise_in_bounds")
        out = jnp.where(tile == k, got, out)
    return out


def start_copies(pairs, sems):
    copies = [pltpu.make_async_copy(a, b, sems.at[n]) for n, (a, b) in enumerate(pairs)]
    for copy in copies:
        copy.start()
    return copies


def group_pairs(group, pairs):
    return range(2 * group, min(2 * group + 2, pairs))


def turn(x):
    half = x * math.pi
    sq = half * half
    sine = -1.0 / 39916800
    for c in (1.0 / 362880, -1.0 / 5040, 1.0 / 120, -1.0 / 6, 1.0):
        sine = sine * sq + c
    sine = sine * half
    cosine = 1.0 / 479001600
    for c in (-1.0 / 3628800, 1.0 / 40320, -1.0 / 720, 1.0 / 24, -0.5, 1.0):
        cosine = cosine * sq + c
    return 1.0 - 2.0 * sine * sine, 2.0 * sine * cosine


def fill_perm(perm):
    for block in range(0, 512, 256):
        row = iota((256, 512), 0)
        target = (row & 3) * 128 + (block // 256) * 64 + (row >> 2)
        hit = target == iota((256, 512), 1)
        perm[block : block + 256, :] = jnp.where(hit, 1.0, 0.0).astype(BF16)


def wave_table(wave_rows_ref, blocks):
    lane = iota((8, 128), 1)
    row = iota((8, 128), 0)
    index = (lane & 63) * (2 * blocks) + 2 * jnp.minimum(row, blocks - 1) + (lane >> 6)
    return pick(wave_rows_ref, 0, blocks, index)


def fill_tables(table, rotors, wave_rows_ref, lato_ref, active_ref, weight_ref):
    lat_here = table.shape[0]
    blocks = wave_rows_ref.shape[0]
    half = blocks * 128
    row = iota((8, 128), 0)
    waves = wave_table(wave_rows_ref, blocks)
    waves_f = waves.astype(F32)
    steps_low = row.astype(F32)
    steps_high = jnp.where(row == 0, 8.0, jnp.where(row == 1, 128.0, 256.0))
    first_slot = (lax.axis_index("wide") * lax.axis_size("lev") + lax.axis_index("lev")) * lat_here
    for i in range(lat_here):
        lat = lato_ref[first_slot + i]
        live = jnp.full((8, 128), active_ref[lat], I32)
        cells = (live * 4).astype(F32)
        inverse = 1.0 / cells
        gain = jnp.full((8, 128), weight_ref[lat], F32) / cells
        for p in range(blocks):
            wave = jnp.broadcast_to(waves_f[p : p + 1, :], (8, 128))
            alive = jnp.broadcast_to(waves[p : p + 1, :], (8, 128)) < live
            angles = []
            for steps in (steps_low, steps_high):
                phase = wave * steps
                rest = phase - jnp.round(phase * inverse) * cells
                angles.append(turn(rest * inverse))
            (cos_b, sin_b), (cos_h, sin_h) = angles
            cos8 = jnp.broadcast_to(cos_h[0:1, :], (8, 128))
            sin8 = jnp.broadcast_to(sin_h[0:1, :], (8, 128))
            lo, hi = p * 128, half + p * 128
            held = []
            for b in range(16):
                held.append((cos_b, sin_b))
                if b % 2:
                    at = (b - 1) * 8
                    table[i, at : at + 16, lo : lo + 128] = jnp.concatenate(
                        [held[b - 1][0], cos_b], 0
                    ).astype(BF16)
                    table[i, at : at + 16, hi : hi + 128] = jnp.concatenate(
                        [held[b - 1][1], sin_b], 0
                    ).astype(BF16)
                if b < 15:
                    cos_b, sin_b = cos_b * cos8 - sin_b * sin8, sin_b * cos8 + cos_b * sin8
            scale = jnp.where(alive, jnp.where(wave == 0.0, 1.0, 2.0), 0.0)
            lines = (
                cos_h[1:2, :], sin_h[1:2, :], cos_h[2:3, :], sin_h[2:3, :],
                scale[0:1, :], jnp.where(alive, gain, 0.0)[0:1, :], cells[0:1, :],
            )
            at = (i * blocks + p) * 8
            for n, line in enumerate(lines):
                rotors[at + n : at + n + 1, :] = line


def inverse_kernel(
    wave_hbm, spec_hbm, lat_rows_hbm, leg_hbm,
    out_ref,
    wave_ref, spec_ref, lat_rows_ref, leg, stack, small_sems, sems,
):
    pairs, coef, lat_total = leg.shape
    lat_here = lat_total // 256
    small = start_copies(
        ((lat_rows_hbm, lat_rows_ref), (spec_hbm, spec_ref), (wave_hbm, wave_ref)), small_sems
    )
    copies = start_copies([(leg_hbm.at[p], leg.at[p]) for p in range(pairs)], sems)
    stack[120:128, :] = jnp.zeros((8, 256), F32)
    for copy in small:
        copy.wait()
    table = latitude_table(lat_rows_ref, lat_here)
    wide = lax.axis_index("wide")
    column = iota((2, coef), 1)
    lefts = []
    for p in range(pairs):
        own = column < coef - 1 - wave_ref[wide * 2 * pairs + 2 * p]
        rows = spec_ref[p].astype(F32)
        nothing = jnp.zeros_like(rows)
        used = [jnp.where(own, rows, nothing), jnp.where(own, nothing, rows)]
        idle = [nothing, nothing]
        lefts.append(jnp.concatenate(idle + used if p % 2 else used + idle, 0).astype(BF16))
    for group in range((pairs + 1) // 2):
        total = jnp.zeros((8, lat_total), F32)
        for p in group_pairs(group, pairs):
            copies[p].wait()
            total = total + jnp.dot(lefts[p], leg[p], preferred_element_type=F32)
        total = total.astype(BF16).astype(F32)
        tiles = [total[:, k * 128 : (k + 1) * 128] for k in range(lat_total // 128)]
        for i in range(lat_here):
            at = i * 24 + group * 8
            for h in range(2):
                index = jnp.broadcast_to(table[i : i + 1, h * 128 : (h + 1) * 128], (8, 128))
                stack[at : at + 8, h * 128 : (h + 1) * 128] = gather_tiles(tiles, index)
    out_ref[...] = stack[...].T


def prepare_kernel(
    wave_hbm, wave_rows_hbm, lat_hbm, lat_rows_hbm, active_hbm, weight_hbm, leg_hbm,
    table, rotors, perm, position, owners, turned_hbm,
    wave_ref, wave_rows_ref, lat_ref, lat_rows_ref, active_ref, weight_ref, leg, turned,
    small_sems, load_sems, store_sems,
):
    lat_here = table.shape[0]
    pairs, coef, lat_total = leg.shape
    copies = start_copies(
        (
            (lat_rows_hbm, lat_rows_ref),
            (wave_rows_hbm, wave_rows_ref),
            (wave_hbm, wave_ref),
            (lat_hbm, lat_ref),
            (active_hbm, active_ref),
            (weight_hbm, weight_ref),
        ),
        small_sems,
    )
    loads = start_copies([(leg_hbm.at[p], leg.at[p]) for p in range(pairs)], load_sems)
    fill_perm(perm)
    for copy in copies:
        copy.wait()
    fill_tables(table, rotors, wave_rows_ref, lat_ref, active_ref, weight_ref)
    where_from = latitude_table(lat_rows_ref, lat_here)
    lanes = iota((128, 128), 1).astype(F32)
    position[...] = jnp.zeros_like(position)
    for block in range(lat_here * 2):
        latitude = iota((128, 128), 0) + block * 128
        found = jnp.zeros((128, 128), F32)
        for i in range(lat_here):
            for h in range(2):
                row = where_from[i : i + 1, h * 128 : (h + 1) * 128]
                hit = jnp.broadcast_to(row, (128, 128)) == latitude
                found = jnp.where(hit, lanes + (i * 256 + h * 128), found)
        total = jnp.sum(found.T, axis=0, keepdims=True)
        position[block : block + 1, :] = total.astype(I32)
    wide = lax.axis_index("wide")
    column = iota((1, owners.shape[1]), 1)
    owners[...] = jnp.zeros_like(owners)
    for p in range(pairs):
        own = column < coef - 1 - wave_ref[wide * 2 * pairs + 2 * p]
        owners[p : p + 1, :] = jnp.where(own, 1.0, 0.0)
    stores = []
    for p in range(pairs):
        loads[p].wait()
        for at in range(0, coef, 128):
            if at + 128 <= coef:
                block = leg[p, at : at + 128, :]
            else:
                block = jnp.broadcast_to(leg[p, at : at + 1, :], (128, lat_total))
            turned[p, :, at : at + 128] = block.T
        stores += start_copies(
            [(turned.at[p], turned_hbm.at[p])], store_sems.at[pl.ds(p, 1)]
        )
    for copy in stores:
        copy.wait()


def direct_kernel(recv_ref, position, owners, turned, out_ref):
    pairs, _, _, coef = out_ref.shape
    lat_total = turned.shape[1]
    lat_here = lat_total // 256
    rows = recv_ref[...].T
    for group in range((pairs + 1) // 2):
        tiles = []
        for i in range(lat_here):
            at = i * 24 + group * 8
            tiles += [rows[at : at + 8, :128], rows[at : at + 8, 128:]]
        ordered = []
        for block in range(lat_total // 128):
            index = jnp.broadcast_to(position[block : block + 1, :], (8, 128))
            ordered.append(gather_tiles(tiles, index))
        left = jnp.concatenate(ordered, 1).astype(BF16)
        for p in group_pairs(group, pairs):
            own = owners[p : p + 1, :coef] > 0.0
            result = jnp.dot(left, turned[p], preferred_element_type=F32)
            at = 4 * (p % 2)
            for r in range(2):
                out_ref[p, r, :, :] = jnp.where(
                    own,
                    result[at + r : at + r + 1, :coef],
                    result[at + 2 + r : at + 3 + r, :coef],
                )


def fourier_kernel(
    recv_ref, table, rotors, perm, wind_ref, grid_hbm, out_ref,
    flat, four, left, backs, grid_ref, sems,
):
    lat_here, levels, points = wind_ref.shape
    half = table.shape[2] // 2
    blocks = half // 128
    outer = points // 128
    for h in range(2):
        flat[h * 128 : (h + 1) * 128, :] = recv_ref[h * 128 : (h + 1) * 128, :].T
    joined = jnp.concatenate(
        [
            jnp.concatenate(
                [
                    flat[pl.ds(h * 128 + 2 * s + r, 32, stride=4), :]
                    for s in range(2)
                    for h in range(2)
                ],
                1,
            )
            for r in range(2)
        ],
        0,
    ).astype(BF16)
    spread = jnp.dot(joined, perm[...], preferred_element_type=F32)
    for l in range(4):
        for copy in range(2):
            four[pl.ds(copy * 4 + l, 64, stride=8), :] = spread[:, l * 128 : (l + 1) * 128]
    backs[...] = jnp.zeros_like(backs)
    upper = iota((8, 128), 0) < 4
    outer_row = iota((outer * 4, 128), 0) >> 2
    point = (outer_row * 128 + iota((outer * 4, 128), 1)).astype(F32)

    def rotor(i, p, n):
        at = (i * blocks + p) * 8 + n
        return jnp.broadcast_to(rotors[at : at + 1, :], (8, 128))

    copies = []
    for i in range(lat_here):
        for p in range(blocks):
            cosx = jnp.where(upper, 1.0, rotor(i, p, 0))
            sinx = jnp.where(upper, 0.0, rotor(i, p, 1))
            cos2, sin2, scale = (rotor(i, p, n) for n in (2, 3, 4))
            lo, hi = p * 128, half + p * 128
            at = (i * 6 + p) * 8
            real = four[at : at + 8, :] * scale
            at = (32 + i * 6 + p) * 8
            imag = four[at : at + 8, :] * scale
            real, imag = real * cosx - imag * sinx, real * sinx + imag * cosx
            held = []
            for a in range(outer // 2):
                held.append((real, imag))
                if a % 2:
                    at = (a - 1) * 8
                    left[i, at : at + 16, lo : lo + 128] = jnp.concatenate(
                        [held[a - 1][0], real], 0
                    ).astype(BF16)
                    left[i, at : at + 16, hi : hi + 128] = -jnp.concatenate(
                        [held[a - 1][1], imag], 0
                    ).astype(BF16)
                if a < outer // 2 - 1:
                    real, imag = real * cos2 - imag * sin2, real * sin2 + imag * cos2
        values = lax.dot_general(left[i], table[i], NT, preferred_element_type=F32)
        cells = jnp.broadcast_to(rotors[i * blocks * 8 + 6 : i * blocks * 8 + 7, :], point.shape)
        values = jnp.where(point < cells, values, 0.0).astype(BF16).astype(F32)
        winds = []
        for a in range(outer):
            grid_ref[i, :, a * 128 : (a + 1) * 128] = values[a * 4 : a * 4 + 4, :].astype(BF16)
            winds.append(wind_ref[i, :, a * 128 : (a + 1) * 128].astype(F32))
        copies += start_copies([(grid_ref.at[i], grid_hbm.at[i])], sems.at[pl.ds(i, 1)])
        product = (values * jnp.concatenate(winds, 0)).astype(BF16)
        sums = jnp.dot(product, table[i], preferred_element_type=F32)
        for p in range(blocks):
            cosx = jnp.where(upper, 1.0, rotor(i, p, 0))
            sinx = jnp.where(upper, 0.0, rotor(i, p, 1))
            cos2, sin2, gain = (rotor(i, p, n) for n in (2, 3, 5))
            lo, hi = p * 128, half + p * 128
            last = outer * 4 - 8
            real = sums[last : last + 8, lo : lo + 128]
            imag = sums[last : last + 8, hi : hi + 128]
            for at in range(last - 8, -1, -8):
                real, imag = (
                    sums[at : at + 8, lo : lo + 128] + (real * cos2 - imag * sin2),
                    sums[at : at + 8, hi : hi + 128] + (real * sin2 + imag * cos2),
                )
            real, imag = real * cosx - imag * sinx, real * sinx + imag * cosx
            real = real + pltpu.roll(real, 4, 0)
            imag = imag + pltpu.roll(imag, 4, 0)
            both = jnp.where(upper, real, -imag) * gain
            at = (i * 6 + p) * 4
            backs[at : at + 4, :] = both[0:4, :]
            at = (32 + i * 6 + p) * 4
            backs[at : at + 4, :] = both[4:8, :]

    joined = jnp.concatenate([backs[pl.ds(l, 64, stride=4), :] for l in range(4)], 1)
    spread = lax.dot_general(joined.astype(BF16), perm[...], NT, preferred_element_type=F32)
    for r in range(2):
        for s in range(2):
            for h in range(2):
                lo = s * 256 + h * 128
                flat[pl.ds(h * 128 + 2 * s + r, 32, stride=4), :] = spread[
                    r * 32 : r * 32 + 32, lo : lo + 128
                ]
    for h in range(2):
        out_ref[h * 128 : (h + 1) * 128, :] = flat[h * 128 : (h + 1) * 128, :].T
    for copy in copies:
        copy.wait()


def vmem():
    return pl.BlockSpec(memory_space=pltpu.VMEM)


def hbm():
    return pl.BlockSpec(memory_space=pltpu.HBM)


def in_hbm(x):
    return pltpu.with_memory_space_constraint(x, pltpu.HBM)


def exchange(rows):
    count, width = rows.shape
    moved = lax.all_to_all(
        rows.reshape(count, 1, width), ("wide", "lev"), split_axis=0, concat_axis=0, tiled=True
    )
    return moved.reshape(count, width)


def shards(spec_in, legendre, wind, lat_weight, wave_order, lat_order, active):
    pairs, coef, lat_total = legendre.shape
    lat_here, levels, points = wind.shape
    devices = lat_total // lat_here
    limit = pltpu.CompilerParams(vmem_limit_bytes=24 * 1024 * 1024)
    lat_rows = lat_order.reshape(lat_total // 128, 128)
    wave_rows = wave_order.reshape(wave_order.shape[0] // 128, 128)

    waves = wave_order.shape[0]
    wide_coef = (coef + 127) // 128 * 128
    operands = (wave_order, spec_in.reshape(pairs, 2, coef), lat_rows, legendre)
    outgoing = pl.pallas_call(
        inverse_kernel,
        name="legendre_inverse",
        out_shape=jax.ShapeDtypeStruct((devices, 128), F32),
        in_specs=[hbm()] * len(operands),
        out_specs=vmem(),
        scratch_shapes=[
            pltpu.SMEM(wave_order.shape, I32),
            pltpu.VMEM((pairs, 2, coef), BF16),
            pltpu.VMEM(lat_rows.shape, I32),
            pltpu.VMEM(legendre.shape, BF16),
            pltpu.VMEM((128, devices), F32),
            pltpu.SemaphoreType.DMA((3,)),
            pltpu.SemaphoreType.DMA((pairs,)),
        ],
        compiler_params=limit,
    )(*(in_hbm(x) for x in operands))

    arrived = exchange(outgoing)
    operands = (wave_order, wave_rows, lat_order, lat_rows, active, lat_weight, legendre)
    table, rotors, perm, position, owners, turned = pl.pallas_call(
        prepare_kernel,
        name="prepare",
        out_shape=(
            jax.ShapeDtypeStruct((lat_here, 128, 2 * waves), BF16),
            jax.ShapeDtypeStruct((lat_here * waves // 128 * 8, 128), F32),
            jax.ShapeDtypeStruct((512, 512), BF16),
            jax.ShapeDtypeStruct((16, 128), I32),
            jax.ShapeDtypeStruct((8, wide_coef), F32),
            pltpu.HBM((pairs, lat_total, wide_coef), BF16),
        ),
        in_specs=[hbm()] * len(operands),
        out_specs=(vmem(),) * 5 + (hbm(),),
        scratch_shapes=[
            pltpu.SMEM(wave_order.shape, I32),
            pltpu.VMEM(wave_rows.shape, I32),
            pltpu.SMEM(lat_order.shape, I32),
            pltpu.VMEM(lat_rows.shape, I32),
            pltpu.SMEM(active.shape, I32),
            pltpu.SMEM(lat_weight.shape, F32),
            pltpu.VMEM(legendre.shape, BF16),
            pltpu.VMEM((pairs, lat_total, wide_coef), BF16),
            pltpu.SemaphoreType.DMA((6,)),
            pltpu.SemaphoreType.DMA((pairs,)),
            pltpu.SemaphoreType.DMA((pairs,)),
        ],
        compiler_params=limit,
        cost_estimate=BUSY,
    )(*(in_hbm(x) for x in operands))

    grid, outgoing = pl.pallas_call(
        fourier_kernel,
        name="fourier",
        out_shape=(
            jax.ShapeDtypeStruct(wind.shape, BF16),
            jax.ShapeDtypeStruct((devices, 128), F32),
        ),
        in_specs=[vmem()] * 5,
        out_specs=(hbm(), vmem()),
        scratch_shapes=[
            pltpu.VMEM((devices, 128), F32),
            pltpu.VMEM((512, 128), F32),
            pltpu.VMEM((lat_here, points // 32, 2 * waves), BF16),
            pltpu.VMEM((256, 128), F32),
            pltpu.VMEM(wind.shape, BF16),
            pltpu.SemaphoreType.DMA((lat_here,)),
        ],
        compiler_params=limit,
        cost_estimate=BUSY,
    )(arrived, table, rotors, perm, wind)

    arrived = exchange(outgoing)
    spec_out = pl.pallas_call(
        direct_kernel,
        name="legendre_direct",
        out_shape=jax.ShapeDtypeStruct((pairs, 2, 1, coef), F32),
        in_specs=[vmem()] * 4,
        out_specs=vmem(),
        compiler_params=limit,
    )(arrived, position, owners, turned)
    return (grid, spec_out)


def solution(mesh):
    in_specs = (
        P("wide", None, "lev", None),
        P("wide", None, None),
        P(("wide", "lev"), None, None),
        P(),
        P(),
        P(),
        P(),
    )
    out_specs = (P(("wide", "lev"), None, None), P("wide", None, "lev", None))
    return jax.shard_map(shards, mesh=mesh, in_specs=in_specs, out_specs=out_specs, check_vma=False)
```

```python
import math

import jax
import jax.numpy as jnp
from jax import lax
from jax.experimental import pallas as pl
from jax.experimental.pallas import tpu as pltpu
from jax.sharding import PartitionSpec as P

F32 = jnp.float32
BF16 = jnp.bfloat16
I32 = jnp.int32
NT = (((1,), (1,)), ((), ()))
FLIGHT = 5


def iota(shape, axis):
    return lax.broadcasted_iota(I32, shape, axis)


def pick(table_ref, first_row, row_count, index):
    row = index >> 7
    lane = index & 127
    out = jnp.zeros(index.shape, I32)
    for k in range(row_count):
        line = jnp.broadcast_to(table_ref[first_row + k : first_row + k + 1, :], index.shape)
        got = jnp.take_along_axis(line, lane, axis=1, mode="promise_in_bounds")
        out = jnp.where(row == k, got, out)
    return out


def latitude_table(lat_ref, lat_here):
    halves = []
    index = iota((8, 128), 1) * lat_here + jnp.minimum(iota((8, 128), 0), lat_here - 1)
    for h in range(2):
        halves.append(pick(lat_ref, h * lat_here, lat_here, index))
    return jnp.concatenate(halves, 1)


def gather_tiles(tiles, index):
    tile = index >> 7
    lane = index & 127
    out = jnp.zeros(index.shape, tiles[0].dtype)
    for k, source in enumerate(tiles):
        got = jnp.take_along_axis(source, lane, axis=1, mode="promise_in_bounds")
        out = jnp.where(tile == k, got, out)
    return out


def start_copies(pairs, sems):
    copies = [pltpu.make_async_copy(a, b, sems.at[n]) for n, (a, b) in enumerate(pairs)]
    for copy in copies:
        copy.start()
    return copies


def group_pairs(group, pairs):
    return range(2 * group, min(2 * group + 2, pairs))


def turn(x):
    half = x * math.pi
    sq = half * half
    sine = -1.0 / 39916800
    for c in (1.0 / 362880, -1.0 / 5040, 1.0 / 120, -1.0 / 6, 1.0):
        sine = sine * sq + c
    sine = sine * half
    cosine = 1.0 / 479001600
    for c in (-1.0 / 3628800, 1.0 / 40320, -1.0 / 720, 1.0 / 24, -0.5, 1.0):
        cosine = cosine * sq + c
    return 1.0 - 2.0 * sine * sine, 2.0 * sine * cosine


def fill_perm(perm):
    for block in range(0, 512, 256):
        row = iota((256, 512), 0)
        target = (row & 3) * 128 + (block // 256) * 64 + (row >> 2)
        hit = target == iota((256, 512), 1)
        perm[block : block + 256, :] = jnp.where(hit, 1.0, 0.0).astype(BF16)


def wave_table(wave_rows_ref, blocks):
    lane = iota((8, 128), 1)
    row = iota((8, 128), 0)
    index = (lane & 63) * (2 * blocks) + 2 * jnp.minimum(row, blocks - 1) + (lane >> 6)
    return pick(wave_rows_ref, 0, blocks, index)


def fill_tables(table, rotors, waves, i, lato_ref, active_ref, weight_ref):
    lat_here = table.shape[0]
    half = table.shape[2] // 2
    blocks = half // 128
    row = iota((8, 128), 0)
    waves_f = waves.astype(F32)
    steps_low = row.astype(F32)
    steps_high = jnp.where(row == 0, 8.0, jnp.where(row == 1, 128.0, 256.0))
    first_slot = (lax.axis_index("wide") * lax.axis_size("lev") + lax.axis_index("lev")) * lat_here
    lat = lato_ref[first_slot + i]
    live = jnp.full((8, 128), active_ref[lat], I32)
    cells = (live * 4).astype(F32)
    inverse = 1.0 / cells
    gain = jnp.full((8, 128), weight_ref[lat], F32) / cells
    for p in range(blocks):
        wave = jnp.broadcast_to(waves_f[p : p + 1, :], (8, 128))
        alive = jnp.broadcast_to(waves[p : p + 1, :], (8, 128)) < live
        angles = []
        for steps in (steps_low, steps_high):
            phase = wave * steps
            rest = phase - jnp.round(phase * inverse) * cells
            angles.append(turn(rest * inverse))
        (cos_b, sin_b), (cos_h, sin_h) = angles
        cos8 = jnp.broadcast_to(cos_h[0:1, :], (8, 128))
        sin8 = jnp.broadcast_to(sin_h[0:1, :], (8, 128))
        lo, hi = p * 128, half + p * 128
        held = []
        for b in range(16):
            held.append((cos_b, sin_b))
            if b % 2:
                at = (b - 1) * 8
                table[i, at : at + 16, lo : lo + 128] = jnp.concatenate(
                    [held[b - 1][0], cos_b], 0
                ).astype(BF16)
                table[i, at : at + 16, hi : hi + 128] = jnp.concatenate(
                    [held[b - 1][1], sin_b], 0
                ).astype(BF16)
            if b < 15:
                cos_b, sin_b = cos_b * cos8 - sin_b * sin8, sin_b * cos8 + cos_b * sin8
        scale = jnp.where(alive, jnp.where(wave == 0.0, 1.0, 2.0), 0.0)
        lines = (
            cos_h[1:2, :], sin_h[1:2, :], cos_h[2:3, :], sin_h[2:3, :],
            scale[0:1, :], jnp.where(alive, gain, 0.0)[0:1, :], cells[0:1, :],
        )
        at = (i * blocks + p) * 8
        for n, line in enumerate(lines):
            rotors[at + n : at + n + 1, :] = line


def fill_position(position, where_from, lat_here):
    rows = jnp.concatenate(
        [where_from[i : i + 1, h * 128 : (h + 1) * 128] for i in range(lat_here) for h in range(2)],
        1,
    )
    count = rows.shape[1]
    number = iota((16, count), 1)
    high = jnp.broadcast_to(rows >> 7, (16, count)) == iota((16, count), 0)
    parts = [
        jnp.where(high, part.astype(F32), 0.0).astype(BF16) for part in (number >> 4, number & 15)
    ]
    low = jnp.broadcast_to(rows & 127, (128, count)) == iota((128, count), 0)
    found = lax.dot_general(
        jnp.concatenate(parts, 0),
        jnp.where(low, 1.0, 0.0).astype(BF16),
        NT,
        preferred_element_type=F32,
    )
    position[...] = (found[:16, :] * 16.0 + found[16:, :]).astype(I32)


def turn_pair(turned, leg, p):
    _, coef, lat_total = leg.shape
    for at in range(0, coef, 128):
        if at + 128 <= coef:
            block = leg[p, at : at + 128, :]
        else:
            block = jnp.broadcast_to(leg[p, at : at + 1, :], (128, lat_total))
        turned[p, :, at : at + 128] = block.T


def inverse_kernel(
    wave_hbm, wave_rows_hbm, spec_hbm, lat_hbm, lat_rows_hbm, active_hbm, weight_hbm, leg_hbm,
    out_ref, leg, table, rotors, perm, position, owners,
    wave_ref, wave_rows_ref, spec_ref, lat_ref, lat_rows_ref, active_ref, weight_ref,
    stack, small_sems, sems,
):
    pairs, coef, lat_total = leg_hbm.shape
    lat_here = lat_total // 256
    small = start_copies(
        (
            (lat_rows_hbm, lat_rows_ref),
            (wave_rows_hbm, wave_rows_ref),
            (wave_hbm, wave_ref),
            (spec_hbm, spec_ref),
            (lat_hbm, lat_ref),
            (active_hbm, active_ref),
            (weight_hbm, weight_ref),
        ),
        small_sems,
    )
    copies = [pltpu.make_async_copy(leg_hbm.at[p], leg.at[p], sems.at[p]) for p in range(pairs)]
    for copy in copies[:FLIGHT]:
        copy.start()
    stack[120:128, :] = jnp.zeros((8, 256), F32)
    fill_perm(perm)
    owners[...] = jnp.zeros_like(owners)
    for copy in small:
        copy.wait()
    where_from = latitude_table(lat_rows_ref, lat_here)
    fill_position(position, where_from, lat_here)
    waves = wave_table(wave_rows_ref, wave_rows_ref.shape[0])
    wide = lax.axis_index("wide")
    column = iota((2, coef), 1)
    lefts = []
    for p in range(pairs):
        own = column < coef - 1 - wave_ref[wide * 2 * pairs + 2 * p]
        owners[p : p + 1, :coef] = jnp.where(own[:1], 1.0, 0.0)
        rows = spec_ref[p].astype(F32)
        nothing = jnp.zeros_like(rows)
        used = [jnp.where(own, rows, nothing), jnp.where(own, nothing, rows)]
        idle = [nothing, nothing]
        lefts.append(jnp.concatenate(idle + used if p % 2 else used + idle, 0).astype(BF16))
    total = None
    for p in range(pairs):
        for i in range(p, lat_here, pairs):
            fill_tables(table, rotors, waves, i, lat_ref, active_ref, weight_ref)
        copies[p].wait()
        if p + FLIGHT < pairs:
            copies[p + FLIGHT].start()
        result = jnp.dot(lefts[p], leg[p], preferred_element_type=F32)
        total = total + result if p % 2 else result
        if p % 2 == 0 and p < pairs - 1:
            continue
        total = total.astype(BF16).astype(F32)
        tiles = [total[:, k * 128 : (k + 1) * 128] for k in range(lat_total // 128)]
        for i in range(lat_here):
            at = i * 24 + p // 2 * 8
            for h in range(2):
                index = jnp.broadcast_to(where_from[i : i + 1, h * 128 : (h + 1) * 128], (8, 128))
                stack[at : at + 8, h * 128 : (h + 1) * 128] = gather_tiles(tiles, index)
    out_ref[...] = stack[...].T


def direct_kernel(recv_ref, position, owners, turned, out_ref):
    pairs, _, _, coef = out_ref.shape
    lat_total = turned.shape[1]
    lat_here = lat_total // 256
    rows = recv_ref[...].T
    for group in range((pairs + 1) // 2):
        tiles = []
        for i in range(lat_here):
            at = i * 24 + group * 8
            tiles += [rows[at : at + 8, :128], rows[at : at + 8, 128:]]
        ordered = []
        for block in range(lat_total // 128):
            index = jnp.broadcast_to(position[block : block + 1, :], (8, 128))
            ordered.append(gather_tiles(tiles, index))
        left = jnp.concatenate(ordered, 1).astype(BF16)
        for p in group_pairs(group, pairs):
            own = owners[p : p + 1, :coef] > 0.0
            result = jnp.dot(left, turned[p], preferred_element_type=F32)
            at = 4 * (p % 2)
            for r in range(2):
                out_ref[p, r, :, :] = jnp.where(
                    own,
                    result[at + r : at + r + 1, :coef],
                    result[at + 2 + r : at + 3 + r, :coef],
                )


def fourier_kernel(
    recv_ref, table, rotors, perm, wind_ref, leg, grid_hbm, out_ref, turned,
    flat, four, left, backs, grid_ref, sems,
):
    lat_here, levels, points = wind_ref.shape
    half = table.shape[2] // 2
    blocks = half // 128
    outer = points // 128
    for h in range(2):
        flat[h * 128 : (h + 1) * 128, :] = recv_ref[h * 128 : (h + 1) * 128, :].T
    joined = jnp.concatenate(
        [
            jnp.concatenate(
                [
                    flat[pl.ds(h * 128 + 2 * s + r, 32, stride=4), :]
                    for s in range(2)
                    for h in range(2)
                ],
                1,
            )
            for r in range(2)
        ],
        0,
    ).astype(BF16)
    spread = jnp.dot(joined, perm[...], preferred_element_type=F32)
    for l in range(4):
        for copy in range(2):
            four[pl.ds(copy * 4 + l, 64, stride=8), :] = spread[:, l * 128 : (l + 1) * 128]
    backs[...] = jnp.zeros_like(backs)
    upper = iota((8, 128), 0) < 4
    outer_row = iota((outer * 4, 128), 0) >> 2
    point = (outer_row * 128 + iota((outer * 4, 128), 1)).astype(F32)

    def rotor(i, p, n):
        at = (i * blocks + p) * 8 + n
        return jnp.broadcast_to(rotors[at : at + 1, :], (8, 128))

    copies = []
    for i in range(lat_here):
        for p in range(blocks):
            cosx = jnp.where(upper, 1.0, rotor(i, p, 0))
            sinx = jnp.where(upper, 0.0, rotor(i, p, 1))
            cos2, sin2, scale = (rotor(i, p, n) for n in (2, 3, 4))
            lo, hi = p * 128, half + p * 128
            at = (i * 6 + p) * 8
            real = four[at : at + 8, :] * scale
            at = (32 + i * 6 + p) * 8
            imag = four[at : at + 8, :] * scale
            real, imag = real * cosx - imag * sinx, real * sinx + imag * cosx
            held = []
            for a in range(outer // 2):
                held.append((real, imag))
                if a % 2:
                    at = (a - 1) * 8
                    left[i, at : at + 16, lo : lo + 128] = jnp.concatenate(
                        [held[a - 1][0], real], 0
                    ).astype(BF16)
                    left[i, at : at + 16, hi : hi + 128] = -jnp.concatenate(
                        [held[a - 1][1], imag], 0
                    ).astype(BF16)
                if a < outer // 2 - 1:
                    real, imag = real * cos2 - imag * sin2, real * sin2 + imag * cos2
        for p in range(i, leg.shape[0], lat_here):
            turn_pair(turned, leg, p)
        values = lax.dot_general(left[i], table[i], NT, preferred_element_type=F32)
        cells = jnp.broadcast_to(rotors[i * blocks * 8 + 6 : i * blocks * 8 + 7, :], point.shape)
        values = jnp.where(point < cells, values, 0.0).astype(BF16).astype(F32)
        winds = []
        for a in range(outer):
            grid_ref[i, :, a * 128 : (a + 1) * 128] = values[a * 4 : a * 4 + 4, :].astype(BF16)
            winds.append(wind_ref[i, :, a * 128 : (a + 1) * 128].astype(F32))
        copies += start_copies([(grid_ref.at[i], grid_hbm.at[i])], sems.at[pl.ds(i, 1)])
        product = (values * jnp.concatenate(winds, 0)).astype(BF16)
        sums = jnp.dot(product, table[i], preferred_element_type=F32)
        for p in range(blocks):
            cosx = jnp.where(upper, 1.0, rotor(i, p, 0))
            sinx = jnp.where(upper, 0.0, rotor(i, p, 1))
            cos2, sin2, gain = (rotor(i, p, n) for n in (2, 3, 5))
            lo, hi = p * 128, half + p * 128
            last = outer * 4 - 8
            real = sums[last : last + 8, lo : lo + 128]
            imag = sums[last : last + 8, hi : hi + 128]
            for at in range(last - 8, -1, -8):
                real, imag = (
                    sums[at : at + 8, lo : lo + 128] + (real * cos2 - imag * sin2),
                    sums[at : at + 8, hi : hi + 128] + (real * sin2 + imag * cos2),
                )
            real, imag = real * cosx - imag * sinx, real * sinx + imag * cosx
            real = real + pltpu.roll(real, 4, 0)
            imag = imag + pltpu.roll(imag, 4, 0)
            both = jnp.where(upper, real, -imag) * gain
            at = (i * 6 + p) * 4
            backs[at : at + 4, :] = both[0:4, :]
            at = (32 + i * 6 + p) * 4
            backs[at : at + 4, :] = both[4:8, :]

    joined = jnp.concatenate([backs[pl.ds(l, 64, stride=4), :] for l in range(4)], 1)
    spread = lax.dot_general(joined.astype(BF16), perm[...], NT, preferred_element_type=F32)
    for r in range(2):
        for s in range(2):
            for h in range(2):
                lo = s * 256 + h * 128
                flat[pl.ds(h * 128 + 2 * s + r, 32, stride=4), :] = spread[
                    r * 32 : r * 32 + 32, lo : lo + 128
                ]
    for h in range(2):
        out_ref[h * 128 : (h + 1) * 128, :] = flat[h * 128 : (h + 1) * 128, :].T
    for copy in copies:
        copy.wait()


def vmem():
    return pl.BlockSpec(memory_space=pltpu.VMEM)


def hbm():
    return pl.BlockSpec(memory_space=pltpu.HBM)


def in_hbm(x):
    return pltpu.with_memory_space_constraint(x, pltpu.HBM)


def exchange(rows):
    count, width = rows.shape
    moved = lax.all_to_all(
        rows.reshape(count, 1, width), ("wide", "lev"), split_axis=0, concat_axis=0, tiled=True
    )
    return moved.reshape(count, width)


def shards(spec_in, legendre, wind, lat_weight, wave_order, lat_order, active):
    pairs, coef, lat_total = legendre.shape
    lat_here, levels, points = wind.shape
    devices = lat_total // lat_here
    limit = pltpu.CompilerParams(vmem_limit_bytes=24 * 1024 * 1024)
    lat_rows = lat_order.reshape(lat_total // 128, 128)
    wave_rows = wave_order.reshape(wave_order.shape[0] // 128, 128)

    waves = wave_order.shape[0]
    wide_coef = (coef + 127) // 128 * 128
    operands = (
        wave_order, wave_rows, spec_in.reshape(pairs, 2, coef), lat_order, lat_rows, active,
        lat_weight, legendre,
    )
    outgoing, leg_here, table, rotors, perm, position, owners = pl.pallas_call(
        inverse_kernel,
        name="legendre_inverse",
        out_shape=(
            jax.ShapeDtypeStruct((devices, 128), F32),
            jax.ShapeDtypeStruct(legendre.shape, BF16),
            jax.ShapeDtypeStruct((lat_here, 128, 2 * waves), BF16),
            jax.ShapeDtypeStruct((lat_here * waves // 128 * 8, 128), F32),
            jax.ShapeDtypeStruct((512, 512), BF16),
            jax.ShapeDtypeStruct((16, 128), I32),
            jax.ShapeDtypeStruct((8, wide_coef), F32),
        ),
        in_specs=[hbm()] * len(operands),
        out_specs=(vmem(),) * 7,
        scratch_shapes=[
            pltpu.SMEM(wave_order.shape, I32),
            pltpu.VMEM(wave_rows.shape, I32),
            pltpu.VMEM((pairs, 2, coef), BF16),
            pltpu.SMEM(lat_order.shape, I32),
            pltpu.VMEM(lat_rows.shape, I32),
            pltpu.SMEM(active.shape, I32),
            pltpu.SMEM(lat_weight.shape, F32),
            pltpu.VMEM((128, devices), F32),
            pltpu.SemaphoreType.DMA((7,)),
            pltpu.SemaphoreType.DMA((pairs,)),
        ],
        compiler_params=limit,
    )(*(in_hbm(x) for x in operands))
    arrived = exchange(outgoing)

    grid, outgoing, turned = pl.pallas_call(
        fourier_kernel,
        name="fourier",
        out_shape=(
            jax.ShapeDtypeStruct(wind.shape, BF16),
            jax.ShapeDtypeStruct((devices, 128), F32),
            jax.ShapeDtypeStruct((pairs, lat_total, wide_coef), BF16),
        ),
        in_specs=[vmem()] * 6,
        out_specs=(hbm(), vmem(), vmem()),
        scratch_shapes=[
            pltpu.VMEM((devices, 128), F32),
            pltpu.VMEM((512, 128), F32),
            pltpu.VMEM((lat_here, points // 32, 2 * waves), BF16),
            pltpu.VMEM((256, 128), F32),
            pltpu.VMEM(wind.shape, BF16),
            pltpu.SemaphoreType.DMA((lat_here,)),
        ],
        compiler_params=limit,
    )(arrived, table, rotors, perm, wind, leg_here)

    arrived = exchange(outgoing)
    spec_out = pl.pallas_call(
        direct_kernel,
        name="legendre_direct",
        out_shape=jax.ShapeDtypeStruct((pairs, 2, 1, coef), F32),
        in_specs=[vmem()] * 4,
        out_specs=vmem(),
        compiler_params=limit,
    )(arrived, position, owners, turned)
    return (grid, spec_out)


def solution(mesh):
    in_specs = (
        P("wide", None, "lev", None),
        P("wide", None, None),
        P(("wide", "lev"), None, None),
        P(),
        P(),
        P(),
        P(),
    )
    out_specs = (P(("wide", "lev"), None, None), P("wide", None, "lev", None))
    return jax.shard_map(shards, mesh=mesh, in_specs=in_specs, out_specs=out_specs, check_vma=False)
```

```python
import math

import jax
import jax.numpy as jnp
from jax import lax
from jax.experimental import pallas as pl
from jax.experimental.pallas import tpu as pltpu
from jax.sharding import PartitionSpec as P

F32 = jnp.float32
BF16 = jnp.bfloat16
I32 = jnp.int32
NT = (((1,), (1,)), ((), ()))


def iota(shape, axis):
    return lax.broadcasted_iota(I32, shape, axis)


def pick(table_ref, first_row, row_count, index):
    row = index >> 7
    lane = index & 127
    out = jnp.zeros(index.shape, I32)
    for k in range(row_count):
        line = jnp.broadcast_to(table_ref[first_row + k : first_row + k + 1, :], index.shape)
        got = jnp.take_along_axis(line, lane, axis=1, mode="promise_in_bounds")
        out = jnp.where(row == k, got, out)
    return out


def latitude_table(lat_ref, lat_here):
    halves = []
    index = iota((8, 128), 1) * lat_here + jnp.minimum(iota((8, 128), 0), lat_here - 1)
    for h in range(2):
        halves.append(pick(lat_ref, h * lat_here, lat_here, index))
    return jnp.concatenate(halves, 1)


def gather_tiles(tiles, index):
    tile = index >> 7
    lane = index & 127
    out = jnp.zeros(index.shape, tiles[0].dtype)
    for k, source in enumerate(tiles):
        got = jnp.take_along_axis(source, lane, axis=1, mode="promise_in_bounds")
        out = jnp.where(tile == k, got, out)
    return out


def start_copies(pairs, sems):
    copies = [pltpu.make_async_copy(a, b, sems.at[n]) for n, (a, b) in enumerate(pairs)]
    for copy in copies:
        copy.start()
    return copies


def group_pairs(group, pairs):
    return range(2 * group, min(2 * group + 2, pairs))


def turn(x):
    half = x * math.pi
    sq = half * half
    sine = -1.0 / 39916800
    for c in (1.0 / 362880, -1.0 / 5040, 1.0 / 120, -1.0 / 6, 1.0):
        sine = sine * sq + c
    sine = sine * half
    cosine = 1.0 / 479001600
    for c in (-1.0 / 3628800, 1.0 / 40320, -1.0 / 720, 1.0 / 24, -0.5, 1.0):
        cosine = cosine * sq + c
    return 1.0 - 2.0 * sine * sine, 2.0 * sine * cosine


def fill_perm(perm):
    for block in range(0, 512, 256):
        row = iota((256, 512), 0)
        target = (row & 3) * 128 + (block // 256) * 64 + (row >> 2)
        hit = target == iota((256, 512), 1)
        perm[block : block + 256, :] = jnp.where(hit, 1.0, 0.0).astype(BF16)


def wave_table(wave_rows_ref, blocks):
    lane = iota((8, 128), 1)
    row = iota((8, 128), 0)
    index = (lane & 63) * (2 * blocks) + 2 * jnp.minimum(row, blocks - 1) + (lane >> 6)
    return pick(wave_rows_ref, 0, blocks, index)


def fill_tables(table, rotors, waves, i, lato_ref, active_ref, weight_ref):
    lat_here = table.shape[0]
    half = table.shape[2] // 2
    blocks = half // 128
    row = iota((8, 128), 0)
    waves_f = waves.astype(F32)
    steps_low = row.astype(F32)
    steps_high = jnp.where(row == 0, 8.0, jnp.where(row == 1, 128.0, 256.0))
    first_slot = (lax.axis_index("wide") * lax.axis_size("lev") + lax.axis_index("lev")) * lat_here
    lat = lato_ref[first_slot + i]
    live = jnp.full((8, 128), active_ref[lat], I32)
    cells = (live * 4).astype(F32)
    inverse = 1.0 / cells
    gain = jnp.full((8, 128), weight_ref[lat], F32) / cells
    for p in range(blocks):
        wave = jnp.broadcast_to(waves_f[p : p + 1, :], (8, 128))
        alive = jnp.broadcast_to(waves[p : p + 1, :], (8, 128)) < live
        angles = []
        for steps in (steps_low, steps_high):
            phase = wave * steps
            rest = phase - jnp.round(phase * inverse) * cells
            angles.append(turn(rest * inverse))
        (cos_b, sin_b), (cos_h, sin_h) = angles
        cos8 = jnp.broadcast_to(cos_h[0:1, :], (8, 128))
        sin8 = jnp.broadcast_to(sin_h[0:1, :], (8, 128))
        lo, hi = p * 128, half + p * 128
        held = []
        for b in range(16):
            held.append((cos_b, sin_b))
            if b % 2:
                at = (b - 1) * 8
                table[i, at : at + 16, lo : lo + 128] = jnp.concatenate(
                    [held[b - 1][0], cos_b], 0
                ).astype(BF16)
                table[i, at : at + 16, hi : hi + 128] = jnp.concatenate(
                    [held[b - 1][1], sin_b], 0
                ).astype(BF16)
            if b < 15:
                cos_b, sin_b = cos_b * cos8 - sin_b * sin8, sin_b * cos8 + cos_b * sin8
        scale = jnp.where(alive, jnp.where(wave == 0.0, 1.0, 2.0), 0.0)
        lines = (
            cos_h[1:2, :], sin_h[1:2, :], cos_h[2:3, :], sin_h[2:3, :],
            scale[0:1, :], jnp.where(alive, gain, 0.0)[0:1, :], cells[0:1, :],
        )
        at = (i * blocks + p) * 8
        for n, line in enumerate(lines):
            rotors[at + n : at + n + 1, :] = line


def fill_position(position, where_from, lat_here):
    rows = jnp.concatenate(
        [where_from[i : i + 1, h * 128 : (h + 1) * 128] for i in range(lat_here) for h in range(2)],
        1,
    )
    count = rows.shape[1]
    number = iota((16, count), 1)
    high = jnp.broadcast_to(rows >> 7, (16, count)) == iota((16, count), 0)
    parts = [
        jnp.where(high, part.astype(F32), 0.0).astype(BF16) for part in (number >> 4, number & 15)
    ]
    low = jnp.broadcast_to(rows & 127, (128, count)) == iota((128, count), 0)
    found = lax.dot_general(
        jnp.concatenate(parts, 0),
        jnp.where(low, 1.0, 0.0).astype(BF16),
        NT,
        preferred_element_type=F32,
    )
    position[...] = (found[:16, :] * 16.0 + found[16:, :]).astype(I32)


def turn_pair(turned, leg, p):
    for at in range(0, leg.shape[1] - 1, 128):
        turned[p, :, at : at + 128] = leg[p, at : at + 128, :].T


def inverse_kernel(
    wave_hbm, wave_rows_hbm, spec_hbm, lat_hbm, lat_rows_hbm, active_hbm, weight_hbm, leg_hbm,
    out_ref, leg, last_rows, table, rotors, perm, position, owners,
    wave_ref, wave_rows_ref, spec_ref, lat_ref, lat_rows_ref, active_ref, weight_ref,
    stack, small_sems, sems,
):
    pairs, coef, lat_total = leg_hbm.shape
    lat_here = lat_total // 256
    small = start_copies(
        (
            (lat_rows_hbm, lat_rows_ref),
            (wave_rows_hbm, wave_rows_ref),
            (wave_hbm, wave_ref),
            (spec_hbm, spec_ref),
            (lat_hbm, lat_ref),
            (active_hbm, active_ref),
            (weight_hbm, weight_ref),
        ),
        small_sems,
    )
    copies = start_copies([(leg_hbm.at[p], leg.at[p]) for p in range(pairs)], sems)
    stack[120:128, :] = jnp.zeros((8, 256), F32)
    fill_perm(perm)
    owners[...] = jnp.zeros_like(owners)
    last_rows[...] = jnp.zeros_like(last_rows)
    for copy in small:
        copy.wait()
    where_from = latitude_table(lat_rows_ref, lat_here)
    fill_position(position, where_from, lat_here)
    waves = wave_table(wave_rows_ref, wave_rows_ref.shape[0])
    wide = lax.axis_index("wide")
    column = iota((2, coef), 1)
    lefts = []
    for p in range(pairs):
        own = column < coef - 1 - wave_ref[wide * 2 * pairs + 2 * p]
        owners[p : p + 1, :coef] = jnp.where(own[:1], 1.0, 0.0)
        rows = spec_ref[p].astype(F32)
        nothing = jnp.zeros_like(rows)
        used = [jnp.where(own, rows, nothing), jnp.where(own, nothing, rows)]
        idle = [nothing, nothing]
        lefts.append(jnp.concatenate(idle + used if p % 2 else used + idle, 0).astype(BF16))
    total = None
    for p in range(pairs):
        for i in range(p, lat_here, pairs):
            fill_tables(table, rotors, waves, i, lat_ref, active_ref, weight_ref)
        copies[p].wait()
        result = jnp.dot(lefts[p][:, : coef - 1], leg[p, : coef - 1, :], preferred_element_type=F32)
        last = leg[p, coef - 1 : coef, :].astype(F32)
        last_rows[p : p + 1, :] = last
        result = result + lefts[p][:, coef - 1 :].astype(F32) * last
        total = total + result if p % 2 else result
        if p % 2 == 0 and p < pairs - 1:
            continue
        total = total.astype(BF16).astype(F32)
        tiles = [total[:, k * 128 : (k + 1) * 128] for k in range(lat_total // 128)]
        for i in range(lat_here):
            at = i * 24 + p // 2 * 8
            for h in range(2):
                index = jnp.broadcast_to(where_from[i : i + 1, h * 128 : (h + 1) * 128], (8, 128))
                stack[at : at + 8, h * 128 : (h + 1) * 128] = gather_tiles(tiles, index)
    out_ref[...] = stack[...].T


def direct_kernel(recv_ref, position, owners, last_rows, turned, leg, out_ref):
    pairs, _, _, coef = out_ref.shape
    lat_total = turned.shape[1]
    lat_here = lat_total // 256
    rows = recv_ref[...].T
    for group in range((pairs + 1) // 2):
        tiles = []
        for i in range(lat_here):
            at = i * 24 + group * 8
            tiles += [rows[at : at + 8, :128], rows[at : at + 8, 128:]]
        ordered = []
        for block in range(lat_total // 128):
            index = jnp.broadcast_to(position[block : block + 1, :], (8, 128))
            ordered.append(gather_tiles(tiles, index))
        left = jnp.concatenate(ordered, 1).astype(BF16)
        for p in group_pairs(group, pairs):
            own = owners[p : p + 1, :coef] > 0.0
            if p < turned.shape[0]:
                result = jnp.dot(left, turned[p], preferred_element_type=F32)
            else:
                block = leg[p, : coef - 1, :]
                result = lax.dot_general(left, block, NT, preferred_element_type=F32)
            last = jnp.sum(left.astype(F32) * last_rows[p : p + 1, :], axis=1, keepdims=True)
            result = jnp.concatenate([result, jnp.broadcast_to(last, (8, 128))], 1)
            at = 4 * (p % 2)
            for r in range(2):
                out_ref[p, r, :, :] = jnp.where(
                    own,
                    result[at + r : at + r + 1, :coef],
                    result[at + 2 + r : at + 3 + r, :coef],
                )


def fourier_kernel(
    recv_ref, table, rotors, perm, wind_ref, leg, grid_hbm, out_ref, turned,
    flat, four, left, backs, grid_ref, sems,
):
    lat_here, levels, points = wind_ref.shape
    half = table.shape[2] // 2
    blocks = half // 128
    outer = points // 128
    for h in range(2):
        flat[h * 128 : (h + 1) * 128, :] = recv_ref[h * 128 : (h + 1) * 128, :].T
    joined = jnp.concatenate(
        [
            jnp.concatenate(
                [
                    flat[pl.ds(h * 128 + 2 * s + r, 32, stride=4), :]
                    for s in range(2)
                    for h in range(2)
                ],
                1,
            )
            for r in range(2)
        ],
        0,
    ).astype(BF16)
    spread = jnp.dot(joined, perm[...], preferred_element_type=F32)
    for l in range(4):
        for copy in range(2):
            four[pl.ds(copy * 4 + l, 64, stride=8), :] = spread[:, l * 128 : (l + 1) * 128]
    backs[...] = jnp.zeros_like(backs)
    upper = iota((8, 128), 0) < 4
    outer_row = iota((outer * 4, 128), 0) >> 2
    point = (outer_row * 128 + iota((outer * 4, 128), 1)).astype(F32)

    def rotor(i, p, n):
        at = (i * blocks + p) * 8 + n
        return jnp.broadcast_to(rotors[at : at + 1, :], (8, 128))

    copies = []
    fields, sums_of = {}, {}

    def inverse_stage(i):
        for p in range(blocks):
            cosx = jnp.where(upper, 1.0, rotor(i, p, 0))
            sinx = jnp.where(upper, 0.0, rotor(i, p, 1))
            cos2, sin2, scale = (rotor(i, p, n) for n in (2, 3, 4))
            lo, hi = p * 128, half + p * 128
            at = (i * 6 + p) * 8
            real = four[at : at + 8, :] * scale
            at = (32 + i * 6 + p) * 8
            imag = four[at : at + 8, :] * scale
            real, imag = real * cosx - imag * sinx, real * sinx + imag * cosx
            held = []
            for a in range(outer // 2):
                held.append((real, imag))
                if a % 2:
                    at = (a - 1) * 8
                    left[i, at : at + 16, lo : lo + 128] = jnp.concatenate(
                        [held[a - 1][0], real], 0
                    ).astype(BF16)
                    left[i, at : at + 16, hi : hi + 128] = -jnp.concatenate(
                        [held[a - 1][1], imag], 0
                    ).astype(BF16)
                if a < outer // 2 - 1:
                    real, imag = real * cos2 - imag * sin2, real * sin2 + imag * cos2
        if i < turned.shape[0]:
            turn_pair(turned, leg, i)
        values = lax.dot_general(left[i], table[i], NT, preferred_element_type=F32)
        cells = jnp.broadcast_to(rotors[i * blocks * 8 + 6 : i * blocks * 8 + 7, :], point.shape)
        values = jnp.where(point < cells, values, 0.0).astype(BF16).astype(F32)
        for a in range(outer):
            grid_ref[i, :, a * 128 : (a + 1) * 128] = values[a * 4 : a * 4 + 4, :].astype(BF16)
        copies.extend(start_copies([(grid_ref.at[i], grid_hbm.at[i])], sems.at[pl.ds(i, 1)]))
        fields[i] = values

    def product_stage(i):
        values = fields[i]
        winds = [
            wind_ref[i, :, a * 128 : (a + 1) * 128].astype(F32) for a in range(outer)
        ]
        product = (values * jnp.concatenate(winds, 0)).astype(BF16)
        sums_of[i] = jnp.dot(product, table[i], preferred_element_type=F32)

    def direct_stage(i):
        sums = sums_of[i]
        for p in range(blocks):
            cosx = jnp.where(upper, 1.0, rotor(i, p, 0))
            sinx = jnp.where(upper, 0.0, rotor(i, p, 1))
            cos2, sin2, gain = (rotor(i, p, n) for n in (2, 3, 5))
            lo, hi = p * 128, half + p * 128
            last = outer * 4 - 8
            real = sums[last : last + 8, lo : lo + 128]
            imag = sums[last : last + 8, hi : hi + 128]
            for at in range(last - 8, -1, -8):
                real, imag = (
                    sums[at : at + 8, lo : lo + 128] + (real * cos2 - imag * sin2),
                    sums[at : at + 8, hi : hi + 128] + (real * sin2 + imag * cos2),
                )
            real, imag = real * cosx - imag * sinx, real * sinx + imag * cosx
            real = real + pltpu.roll(real, 4, 0)
            imag = imag + pltpu.roll(imag, 4, 0)
            both = jnp.where(upper, real, -imag) * gain
            at = (i * 6 + p) * 4
            backs[at : at + 4, :] = both[0:4, :]
            at = (32 + i * 6 + p) * 4
            backs[at : at + 4, :] = both[4:8, :]

    for step in range(lat_here + 2):
        if step < lat_here:
            inverse_stage(step)
        if 1 <= step <= lat_here:
            product_stage(step - 1)
        if step >= 2:
            direct_stage(step - 2)

    joined = jnp.concatenate([backs[pl.ds(l, 64, stride=4), :] for l in range(4)], 1)
    spread = lax.dot_general(joined.astype(BF16), perm[...], NT, preferred_element_type=F32)
    for r in range(2):
        for s in range(2):
            for h in range(2):
                lo = s * 256 + h * 128
                flat[pl.ds(h * 128 + 2 * s + r, 32, stride=4), :] = spread[
                    r * 32 : r * 32 + 32, lo : lo + 128
                ]
    for h in range(2):
        out_ref[h * 128 : (h + 1) * 128, :] = flat[h * 128 : (h + 1) * 128, :].T
    for copy in copies:
        copy.wait()


def vmem():
    return pl.BlockSpec(memory_space=pltpu.VMEM)


def hbm():
    return pl.BlockSpec(memory_space=pltpu.HBM)


def in_hbm(x):
    return pltpu.with_memory_space_constraint(x, pltpu.HBM)


def exchange(rows):
    count, width = rows.shape
    moved = lax.all_to_all(
        rows.reshape(count, 1, width), ("wide", "lev"), split_axis=0, concat_axis=0, tiled=True
    )
    return moved.reshape(count, width)


def shards(spec_in, legendre, wind, lat_weight, wave_order, lat_order, active):
    pairs, coef, lat_total = legendre.shape
    lat_here, levels, points = wind.shape
    devices = lat_total // lat_here
    limit = pltpu.CompilerParams(vmem_limit_bytes=24 * 1024 * 1024)
    lat_rows = lat_order.reshape(lat_total // 128, 128)
    wave_rows = wave_order.reshape(wave_order.shape[0] // 128, 128)

    waves = wave_order.shape[0]
    wide_coef = (coef + 127) // 128 * 128
    operands = (
        wave_order, wave_rows, spec_in.reshape(pairs, 2, coef), lat_order, lat_rows, active,
        lat_weight, legendre,
    )
    outgoing, leg_here, last_rows, table, rotors, perm, position, owners = pl.pallas_call(
        inverse_kernel,
        name="legendre_inverse",
        out_shape=(
            jax.ShapeDtypeStruct((devices, 128), F32),
            jax.ShapeDtypeStruct(legendre.shape, BF16),
            jax.ShapeDtypeStruct((8, lat_total), F32),
            jax.ShapeDtypeStruct((lat_here, 128, 2 * waves), BF16),
            jax.ShapeDtypeStruct((lat_here * waves // 128 * 8, 128), F32),
            jax.ShapeDtypeStruct((512, 512), BF16),
            jax.ShapeDtypeStruct((16, 128), I32),
            jax.ShapeDtypeStruct((8, wide_coef), F32),
        ),
        in_specs=[hbm()] * len(operands),
        out_specs=(vmem(),) * 8,
        scratch_shapes=[
            pltpu.SMEM(wave_order.shape, I32),
            pltpu.VMEM(wave_rows.shape, I32),
            pltpu.VMEM((pairs, 2, coef), BF16),
            pltpu.SMEM(lat_order.shape, I32),
            pltpu.VMEM(lat_rows.shape, I32),
            pltpu.SMEM(active.shape, I32),
            pltpu.SMEM(lat_weight.shape, F32),
            pltpu.VMEM((128, devices), F32),
            pltpu.SemaphoreType.DMA((7,)),
            pltpu.SemaphoreType.DMA((pairs,)),
        ],
        compiler_params=limit,
    )(*(in_hbm(x) for x in operands))
    arrived = exchange(outgoing)

    grid, outgoing, turned = pl.pallas_call(
        fourier_kernel,
        name="fourier",
        out_shape=(
            jax.ShapeDtypeStruct(wind.shape, BF16),
            jax.ShapeDtypeStruct((devices, 128), F32),
            jax.ShapeDtypeStruct((pairs - 1, lat_total, coef - 1), BF16),
        ),
        in_specs=[vmem()] * 6,
        out_specs=(hbm(), vmem(), vmem()),
        scratch_shapes=[
            pltpu.VMEM((devices, 128), F32),
            pltpu.VMEM((512, 128), F32),
            pltpu.VMEM((lat_here, points // 32, 2 * waves), BF16),
            pltpu.VMEM((256, 128), F32),
            pltpu.VMEM(wind.shape, BF16),
            pltpu.SemaphoreType.DMA((lat_here,)),
        ],
        compiler_params=limit,
    )(arrived, table, rotors, perm, wind, leg_here)

    arrived = exchange(outgoing)
    spec_out = pl.pallas_call(
        direct_kernel,
        name="legendre_direct",
        out_shape=jax.ShapeDtypeStruct((pairs, 2, 1, coef), F32),
        in_specs=[vmem()] * 6,
        out_specs=vmem(),
        compiler_params=limit,
    )(arrived, position, owners, last_rows, turned, leg_here)
    return (grid, spec_out)


def solution(mesh):
    in_specs = (
        P("wide", None, "lev", None),
        P("wide", None, None),
        P(("wide", "lev"), None, None),
        P(),
        P(),
        P(),
        P(),
    )
    out_specs = (P(("wide", "lev"), None, None), P("wide", None, "lev", None))
    return jax.shard_map(shards, mesh=mesh, in_specs=in_specs, out_specs=out_specs, check_vma=False)
```

```python
import math

import jax
import jax.numpy as jnp
from jax import lax
from jax.experimental import pallas as pl
from jax.experimental.pallas import tpu as pltpu
from jax.sharding import PartitionSpec as P

F32 = jnp.float32
BF16 = jnp.bfloat16
I32 = jnp.int32
NT = (((1,), (1,)), ((), ()))


def iota(shape, axis):
    return lax.broadcasted_iota(I32, shape, axis)


def pick(table_ref, first_row, row_count, index):
    row = index >> 7
    lane = index & 127
    out = jnp.zeros(index.shape, I32)
    for k in range(row_count):
        line = jnp.broadcast_to(table_ref[first_row + k : first_row + k + 1, :], index.shape)
        got = jnp.take_along_axis(line, lane, axis=1, mode="promise_in_bounds")
        out = jnp.where(row == k, got, out)
    return out


def latitude_table(lat_ref, lat_here):
    halves = []
    index = iota((8, 128), 1) * lat_here + jnp.minimum(iota((8, 128), 0), lat_here - 1)
    for h in range(2):
        halves.append(pick(lat_ref, h * lat_here, lat_here, index))
    return jnp.concatenate(halves, 1)


def gather_tiles(tiles, index):
    tile = index >> 7
    lane = index & 127
    out = jnp.zeros(index.shape, tiles[0].dtype)
    for k, source in enumerate(tiles):
        got = jnp.take_along_axis(source, lane, axis=1, mode="promise_in_bounds")
        out = jnp.where(tile == k, got, out)
    return out


def start_copies(pairs, sems):
    copies = [pltpu.make_async_copy(a, b, sems.at[n]) for n, (a, b) in enumerate(pairs)]
    for copy in copies:
        copy.start()
    return copies


def group_pairs(group, pairs):
    return range(2 * group, min(2 * group + 2, pairs))


def turn(x):
    half = x * math.pi
    sq = half * half
    sine = -1.0 / 39916800
    for c in (1.0 / 362880, -1.0 / 5040, 1.0 / 120, -1.0 / 6, 1.0):
        sine = sine * sq + c
    sine = sine * half
    cosine = 1.0 / 479001600
    for c in (-1.0 / 3628800, 1.0 / 40320, -1.0 / 720, 1.0 / 24, -0.5, 1.0):
        cosine = cosine * sq + c
    return 1.0 - 2.0 * sine * sine, 2.0 * sine * cosine


def fill_perm(perm):
    for block in range(0, 512, 256):
        row = iota((256, 512), 0)
        target = (row & 3) * 128 + (block // 256) * 64 + (row >> 2)
        hit = target == iota((256, 512), 1)
        perm[block : block + 256, :] = jnp.where(hit, 1.0, 0.0).astype(BF16)


def wave_table(wave_rows_ref, blocks):
    lane = iota((8, 128), 1)
    row = iota((8, 128), 0)
    index = (lane & 63) * (2 * blocks) + 2 * jnp.minimum(row, blocks - 1) + (lane >> 6)
    return pick(wave_rows_ref, 0, blocks, index)


def fill_tables(table, rotors, waves, i, lato_ref, active_ref, weight_ref):
    lat_here = table.shape[0]
    half = table.shape[2] // 2
    blocks = half // 128
    row = iota((8, 128), 0)
    waves_f = waves.astype(F32)
    steps_low = row.astype(F32)
    steps_high = jnp.where(row == 0, 8.0, jnp.where(row == 1, 128.0, 256.0))
    first_slot = (lax.axis_index("wide") * lax.axis_size("lev") + lax.axis_index("lev")) * lat_here
    lat = lato_ref[first_slot + i]
    live = jnp.full((8, 128), active_ref[lat], I32)
    cells = (live * 4).astype(F32)
    inverse = 1.0 / cells
    gain = jnp.full((8, 128), weight_ref[lat], F32) / cells
    for p in range(blocks):
        wave = jnp.broadcast_to(waves_f[p : p + 1, :], (8, 128))
        alive = jnp.broadcast_to(waves[p : p + 1, :], (8, 128)) < live
        angles = []
        for steps in (steps_low, steps_high):
            phase = wave * steps
            rest = phase - jnp.round(phase * inverse) * cells
            angles.append(turn(rest * inverse))
        (cos_b, sin_b), (cos_h, sin_h) = angles
        cos8 = jnp.broadcast_to(cos_h[0:1, :], (8, 128))
        sin8 = jnp.broadcast_to(sin_h[0:1, :], (8, 128))
        lo, hi = p * 128, half + p * 128
        held = []
        for b in range(16):
            held.append((cos_b, sin_b))
            if b % 2:
                at = (b - 1) * 8
                table[i, at : at + 16, lo : lo + 128] = jnp.concatenate(
                    [held[b - 1][0], cos_b], 0
                ).astype(BF16)
                table[i, at : at + 16, hi : hi + 128] = jnp.concatenate(
                    [held[b - 1][1], sin_b], 0
                ).astype(BF16)
            if b < 15:
                cos_b, sin_b = cos_b * cos8 - sin_b * sin8, sin_b * cos8 + cos_b * sin8
        scale = jnp.where(alive, jnp.where(wave == 0.0, 1.0, 2.0), 0.0)
        lines = (
            cos_h[1:2, :], sin_h[1:2, :], cos_h[2:3, :], sin_h[2:3, :],
            scale[0:1, :], jnp.where(alive, gain, 0.0)[0:1, :], cells[0:1, :],
        )
        at = (i * blocks + p) * 8
        for n, line in enumerate(lines):
            rotors[at + n : at + n + 1, :] = line


def fill_position(position, where_from, lat_here):
    rows = jnp.concatenate(
        [where_from[i : i + 1, h * 128 : (h + 1) * 128] for i in range(lat_here) for h in range(2)],
        1,
    )
    count = rows.shape[1]
    number = iota((16, count), 1)
    high = jnp.broadcast_to(rows >> 7, (16, count)) == iota((16, count), 0)
    parts = [
        jnp.where(high, part.astype(F32), 0.0).astype(BF16) for part in (number >> 4, number & 15)
    ]
    low = jnp.broadcast_to(rows & 127, (128, count)) == iota((128, count), 0)
    found = lax.dot_general(
        jnp.concatenate(parts, 0),
        jnp.where(low, 1.0, 0.0).astype(BF16),
        NT,
        preferred_element_type=F32,
    )
    position[...] = (found[:16, :] * 16.0 + found[16:, :]).astype(I32)


def turn_pair(turned, leg, p):
    for at in range(0, leg.shape[1] - 1, 128):
        turned[p, :, at : at + 128] = leg[p, at : at + 128, :].T


def inverse_kernel(
    wave_hbm, wave_rows_hbm, spec_hbm, lat_hbm, lat_rows_hbm, active_hbm, weight_hbm, leg_hbm,
    out_ref, leg, last_rows, table, rotors, perm, position, owners,
    wave_ref, wave_rows_ref, spec_ref, lat_ref, lat_rows_ref, active_ref, weight_ref,
    stack, small_sems, sems,
):
    pairs, coef, lat_total = leg_hbm.shape
    lat_here = lat_total // 256
    small = start_copies(
        (
            (lat_rows_hbm, lat_rows_ref),
            (wave_rows_hbm, wave_rows_ref),
            (wave_hbm, wave_ref),
            (spec_hbm, spec_ref),
            (lat_hbm, lat_ref),
            (active_hbm, active_ref),
            (weight_hbm, weight_ref),
        ),
        small_sems,
    )
    copies = start_copies([(leg_hbm.at[p], leg.at[p]) for p in range(pairs)], sems)
    stack[120:128, :] = jnp.zeros((8, 256), F32)
    fill_perm(perm)
    owners[...] = jnp.zeros_like(owners)
    last_rows[...] = jnp.zeros_like(last_rows)
    for copy in small:
        copy.wait()
    where_from = latitude_table(lat_rows_ref, lat_here)
    fill_position(position, where_from, lat_here)
    waves = wave_table(wave_rows_ref, wave_rows_ref.shape[0])
    wide = lax.axis_index("wide")
    column = iota((2, coef), 1)
    lefts = []
    for p in range(pairs):
        own = column < coef - 1 - wave_ref[wide * 2 * pairs + 2 * p]
        owners[p : p + 1, :coef] = jnp.where(own[:1], 1.0, 0.0)
        rows = spec_ref[p].astype(F32)
        nothing = jnp.zeros_like(rows)
        used = [jnp.where(own, rows, nothing), jnp.where(own, nothing, rows)]
        idle = [nothing, nothing]
        lefts.append(jnp.concatenate(idle + used if p % 2 else used + idle, 0).astype(BF16))
    total = None
    for p in range(pairs):
        for i in range(3 * p, min(3 * p + 3, lat_here)):
            fill_tables(table, rotors, waves, i, lat_ref, active_ref, weight_ref)
        copies[p].wait()
        result = jnp.dot(lefts[p][:, : coef - 1], leg[p, : coef - 1, :], preferred_element_type=F32)
        last = leg[p, coef - 1 : coef, :].astype(F32)
        last_rows[p : p + 1, :] = last
        result = result + lefts[p][:, coef - 1 :].astype(F32) * last
        total = total + result if p % 2 else result
        if p % 2 == 0 and p < pairs - 1:
            continue
        total = total.astype(BF16).astype(F32)
        tiles = [total[:, k * 128 : (k + 1) * 128] for k in range(lat_total // 128)]
        for i in range(lat_here):
            at = i * 24 + p // 2 * 8
            for h in range(2):
                index = jnp.broadcast_to(where_from[i : i + 1, h * 128 : (h + 1) * 128], (8, 128))
                stack[at : at + 8, h * 128 : (h + 1) * 128] = gather_tiles(tiles, index)
    out_ref[...] = stack[...].T


def direct_kernel(recv_ref, position, owners, last_rows, turned, leg, out_ref):
    pairs, _, _, coef = out_ref.shape
    lat_total = turned.shape[1]
    lat_here = lat_total // 256
    rows = recv_ref[...].T
    for group in reversed(range((pairs + 1) // 2)):
        tiles = []
        for i in range(lat_here):
            at = i * 24 + group * 8
            tiles += [rows[at : at + 8, :128], rows[at : at + 8, 128:]]
        ordered = []
        for block in range(lat_total // 128):
            index = jnp.broadcast_to(position[block : block + 1, :], (8, 128))
            ordered.append(gather_tiles(tiles, index))
        left = jnp.concatenate(ordered, 1).astype(BF16)
        for p in group_pairs(group, pairs):
            own = owners[p : p + 1, :coef] > 0.0
            if p < turned.shape[0]:
                result = jnp.dot(left, turned[p], preferred_element_type=F32)
            else:
                block = leg[p, : coef - 1, :]
                result = lax.dot_general(left, block, NT, preferred_element_type=F32)
            last = jnp.sum(left.astype(F32) * last_rows[p : p + 1, :], axis=1, keepdims=True)
            result = jnp.concatenate([result, jnp.broadcast_to(last, (8, 128))], 1)
            at = 4 * (p % 2)
            for r in range(2):
                out_ref[p, r, :, :] = jnp.where(
                    own,
                    result[at + r : at + r + 1, :coef],
                    result[at + 2 + r : at + 3 + r, :coef],
                )


def fourier_kernel(
    recv_ref, table, rotors, perm, wind_ref, leg, grid_hbm, out_ref, turned,
    flat, four, left, backs, grid_ref, sems,
):
    lat_here, levels, points = wind_ref.shape
    half = table.shape[2] // 2
    blocks = half // 128
    outer = points // 128
    for h in range(2):
        flat[h * 128 : (h + 1) * 128, :] = recv_ref[h * 128 : (h + 1) * 128, :].T
    joined = jnp.concatenate(
        [
            jnp.concatenate(
                [
                    flat[pl.ds(h * 128 + 2 * s + r, 32, stride=4), :]
                    for s in range(2)
                    for h in range(2)
                ],
                1,
            )
            for r in range(2)
        ],
        0,
    ).astype(BF16)
    spread = jnp.dot(joined, perm[...], preferred_element_type=F32)
    for l in range(4):
        for copy in range(2):
            four[pl.ds(copy * 4 + l, 64, stride=8), :] = spread[:, l * 128 : (l + 1) * 128]
    backs[...] = jnp.zeros_like(backs)
    upper = iota((8, 128), 0) < 4
    outer_row = iota((outer * 4, 128), 0) >> 2
    point = (outer_row * 128 + iota((outer * 4, 128), 1)).astype(F32)

    def rotor(i, p, n):
        at = (i * blocks + p) * 8 + n
        return jnp.broadcast_to(rotors[at : at + 1, :], (8, 128))

    copies = []
    fields, sums_of = {}, {}

    def inverse_stage(i):
        for p in range(blocks):
            cosx = jnp.where(upper, 1.0, rotor(i, p, 0))
            sinx = jnp.where(upper, 0.0, rotor(i, p, 1))
            cos2, sin2, scale = (rotor(i, p, n) for n in (2, 3, 4))
            lo, hi = p * 128, half + p * 128
            at = (i * 6 + p) * 8
            real = four[at : at + 8, :] * scale
            at = (32 + i * 6 + p) * 8
            imag = four[at : at + 8, :] * scale
            real, imag = real * cosx - imag * sinx, real * sinx + imag * cosx
            held = []
            for a in range(outer // 2):
                held.append((real, imag))
                if a % 2:
                    at = (a - 1) * 8
                    left[i, at : at + 16, lo : lo + 128] = jnp.concatenate(
                        [held[a - 1][0], real], 0
                    ).astype(BF16)
                    left[i, at : at + 16, hi : hi + 128] = -jnp.concatenate(
                        [held[a - 1][1], imag], 0
                    ).astype(BF16)
                if a < outer // 2 - 1:
                    real, imag = real * cos2 - imag * sin2, real * sin2 + imag * cos2
        if i < turned.shape[0]:
            turn_pair(turned, leg, i)
        values = lax.dot_general(left[i], table[i], NT, preferred_element_type=F32)
        cells = jnp.broadcast_to(rotors[i * blocks * 8 + 6 : i * blocks * 8 + 7, :], point.shape)
        values = jnp.where(point < cells, values, 0.0).astype(BF16).astype(F32)
        fields[i] = values

    def product_stage(i):
        values = fields[i]
        winds = [
            wind_ref[i, :, a * 128 : (a + 1) * 128].astype(F32) for a in range(outer)
        ]
        product = (values * jnp.concatenate(winds, 0)).astype(BF16)
        sums_of[i] = jnp.dot(product, table[i], preferred_element_type=F32)

    def direct_stage(i):
        sums = sums_of[i]
        values = fields[i]
        for a in range(outer):
            grid_ref[i, :, a * 128 : (a + 1) * 128] = values[a * 4 : a * 4 + 4, :].astype(BF16)
        copies.extend(start_copies([(grid_ref.at[i], grid_hbm.at[i])], sems.at[pl.ds(i, 1)]))
        for p in range(blocks):
            cosx = jnp.where(upper, 1.0, rotor(i, p, 0))
            sinx = jnp.where(upper, 0.0, rotor(i, p, 1))
            cos2, sin2, gain = (rotor(i, p, n) for n in (2, 3, 5))
            lo, hi = p * 128, half + p * 128
            last = outer * 4 - 8
            real = sums[last : last + 8, lo : lo + 128]
            imag = sums[last : last + 8, hi : hi + 128]
            for at in range(last - 8, -1, -8):
                real, imag = (
                    sums[at : at + 8, lo : lo + 128] + (real * cos2 - imag * sin2),
                    sums[at : at + 8, hi : hi + 128] + (real * sin2 + imag * cos2),
                )
            real, imag = real * cosx - imag * sinx, real * sinx + imag * cosx
            real = real + pltpu.roll(real, 4, 0)
            imag = imag + pltpu.roll(imag, 4, 0)
            both = jnp.where(upper, real, -imag) * gain
            at = (i * 6 + p) * 4
            backs[at : at + 4, :] = both[0:4, :]
            at = (32 + i * 6 + p) * 4
            backs[at : at + 4, :] = both[4:8, :]

    for step in range(lat_here + 2):
        if step < lat_here:
            inverse_stage(step)
        if 1 <= step <= lat_here:
            product_stage(step - 1)
        if step >= 2:
            direct_stage(step - 2)

    joined = jnp.concatenate([backs[pl.ds(l, 64, stride=4), :] for l in range(4)], 1)
    spread = lax.dot_general(joined.astype(BF16), perm[...], NT, preferred_element_type=F32)
    for r in range(2):
        for s in range(2):
            for h in range(2):
                lo = s * 256 + h * 128
                flat[pl.ds(h * 128 + 2 * s + r, 32, stride=4), :] = spread[
                    r * 32 : r * 32 + 32, lo : lo + 128
                ]
    for h in range(2):
        out_ref[h * 128 : (h + 1) * 128, :] = flat[h * 128 : (h + 1) * 128, :].T
    for copy in copies:
        copy.wait()


def vmem():
    return pl.BlockSpec(memory_space=pltpu.VMEM)


def hbm():
    return pl.BlockSpec(memory_space=pltpu.HBM)


def in_hbm(x):
    return pltpu.with_memory_space_constraint(x, pltpu.HBM)


def exchange(rows):
    count, width = rows.shape
    moved = lax.all_to_all(
        rows.reshape(count, 1, width), ("wide", "lev"), split_axis=0, concat_axis=0, tiled=True
    )
    return moved.reshape(count, width)


def shards(spec_in, legendre, wind, lat_weight, wave_order, lat_order, active):
    pairs, coef, lat_total = legendre.shape
    lat_here, levels, points = wind.shape
    devices = lat_total // lat_here
    limit = pltpu.CompilerParams(vmem_limit_bytes=24 * 1024 * 1024)
    lat_rows = lat_order.reshape(lat_total // 128, 128)
    wave_rows = wave_order.reshape(wave_order.shape[0] // 128, 128)

    waves = wave_order.shape[0]
    wide_coef = (coef + 127) // 128 * 128
    operands = (
        wave_order, wave_rows, spec_in.reshape(pairs, 2, coef), lat_order, lat_rows, active,
        lat_weight, legendre,
    )
    outgoing, leg_here, last_rows, table, rotors, perm, position, owners = pl.pallas_call(
        inverse_kernel,
        name="legendre_inverse",
        out_shape=(
            jax.ShapeDtypeStruct((devices, 128), F32),
            jax.ShapeDtypeStruct(legendre.shape, BF16),
            jax.ShapeDtypeStruct((8, lat_total), F32),
            jax.ShapeDtypeStruct((lat_here, 128, 2 * waves), BF16),
            jax.ShapeDtypeStruct((lat_here * waves // 128 * 8, 128), F32),
            jax.ShapeDtypeStruct((512, 512), BF16),
            jax.ShapeDtypeStruct((16, 128), I32),
            jax.ShapeDtypeStruct((8, wide_coef), F32),
        ),
        in_specs=[hbm()] * len(operands),
        out_specs=(vmem(),) * 8,
        scratch_shapes=[
            pltpu.SMEM(wave_order.shape, I32),
            pltpu.VMEM(wave_rows.shape, I32),
            pltpu.VMEM((pairs, 2, coef), BF16),
            pltpu.SMEM(lat_order.shape, I32),
            pltpu.VMEM(lat_rows.shape, I32),
            pltpu.SMEM(active.shape, I32),
            pltpu.SMEM(lat_weight.shape, F32),
            pltpu.VMEM((128, devices), F32),
            pltpu.SemaphoreType.DMA((7,)),
            pltpu.SemaphoreType.DMA((pairs,)),
        ],
        compiler_params=limit,
    )(*(in_hbm(x) for x in operands))
    arrived = exchange(outgoing)

    grid, outgoing, turned = pl.pallas_call(
        fourier_kernel,
        name="fourier",
        out_shape=(
            jax.ShapeDtypeStruct(wind.shape, BF16),
            jax.ShapeDtypeStruct((devices, 128), F32),
            jax.ShapeDtypeStruct((pairs - 1, lat_total, coef - 1), BF16),
        ),
        in_specs=[vmem()] * 6,
        out_specs=(hbm(), vmem(), vmem()),
        scratch_shapes=[
            pltpu.VMEM((devices, 128), F32),
            pltpu.VMEM((512, 128), F32),
            pltpu.VMEM((lat_here, points // 32, 2 * waves), BF16),
            pltpu.VMEM((256, 128), F32),
            pltpu.VMEM(wind.shape, BF16),
            pltpu.SemaphoreType.DMA((lat_here,)),
        ],
        compiler_params=limit,
    )(arrived, table, rotors, perm, wind, leg_here)

    arrived = exchange(outgoing)
    spec_out = pl.pallas_call(
        direct_kernel,
        name="legendre_direct",
        out_shape=jax.ShapeDtypeStruct((pairs, 2, 1, coef), F32),
        in_specs=[vmem()] * 6,
        out_specs=vmem(),
        compiler_params=limit,
    )(arrived, position, owners, last_rows, turned, leg_here)
    return (grid, spec_out)


def solution(mesh):
    in_specs = (
        P("wide", None, "lev", None),
        P("wide", None, None),
        P(("wide", "lev"), None, None),
        P(),
        P(),
        P(),
        P(),
    )
    out_specs = (P(("wide", "lev"), None, None), P("wide", None, "lev", None))
    return jax.shard_map(shards, mesh=mesh, in_specs=in_specs, out_specs=out_specs, check_vma=False)
```

```python
import math

import jax
import jax.numpy as jnp
from jax import lax
from jax.experimental import pallas as pl
from jax.experimental.pallas import tpu as pltpu
from jax.sharding import PartitionSpec as P

F32 = jnp.float32
BF16 = jnp.bfloat16
I32 = jnp.int32
NT = (((1,), (1,)), ((), ()))


def iota(shape, axis):
    return lax.broadcasted_iota(I32, shape, axis)


def pick(table_ref, first_row, row_count, index):
    row = index >> 7
    lane = index & 127
    out = jnp.zeros(index.shape, I32)
    for k in range(row_count):
        line = jnp.broadcast_to(table_ref[first_row + k : first_row + k + 1, :], index.shape)
        got = jnp.take_along_axis(line, lane, axis=1, mode="promise_in_bounds")
        out = jnp.where(row == k, got, out)
    return out


def latitude_table(lat_ref, lat_here):
    halves = []
    row = jnp.minimum(iota((8, 128), 0), lat_here - 1)
    for h in range(2):
        device = iota((8, 128), 1) + h * 128
        slot = (((device & 63) << 2) + (device >> 6)) * lat_here + row
        halves.append(pick(lat_ref, 0, lat_ref.shape[0], slot))
    return jnp.concatenate(halves, 1)


def gather_tiles(tiles, index):
    tile = index >> 7
    lane = index & 127
    out = jnp.zeros(index.shape, tiles[0].dtype)
    for k, source in enumerate(tiles):
        got = jnp.take_along_axis(source, lane, axis=1, mode="promise_in_bounds")
        out = jnp.where(tile == k, got, out)
    return out


def start_copies(pairs, sems):
    copies = [pltpu.make_async_copy(a, b, sems.at[n]) for n, (a, b) in enumerate(pairs)]
    for copy in copies:
        copy.start()
    return copies


def group_pairs(group, pairs):
    return range(2 * group, min(2 * group + 2, pairs))


def turn(x):
    half = x * math.pi
    sq = half * half
    sine = -1.0 / 39916800
    for c in (1.0 / 362880, -1.0 / 5040, 1.0 / 120, -1.0 / 6, 1.0):
        sine = sine * sq + c
    sine = sine * half
    cosine = 1.0 / 479001600
    for c in (-1.0 / 3628800, 1.0 / 40320, -1.0 / 720, 1.0 / 24, -0.5, 1.0):
        cosine = cosine * sq + c
    return 1.0 - 2.0 * sine * sine, 2.0 * sine * cosine


def wave_table(wave_rows_ref, blocks):
    lane = iota((8, 128), 1)
    row = iota((8, 128), 0)
    index = (lane & 63) * (2 * blocks) + 2 * jnp.minimum(row, blocks - 1) + (lane >> 6)
    return pick(wave_rows_ref, 0, blocks, index)


def fill_tables(table, rotors, waves, i, lato_ref, active_ref, weight_ref):
    lat_here = table.shape[0]
    half = table.shape[2] // 2
    blocks = half // 128
    row = iota((8, 128), 0)
    waves_f = waves.astype(F32)
    steps_low = row.astype(F32)
    steps_high = jnp.where(row == 0, 8.0, jnp.where(row == 1, 128.0, 256.0))
    first_slot = (lax.axis_index("wide") * lax.axis_size("lev") + lax.axis_index("lev")) * lat_here
    lat = lato_ref[first_slot + i]
    live = jnp.full((8, 128), active_ref[lat], I32)
    cells = (live * 4).astype(F32)
    inverse = 1.0 / cells
    gain = jnp.full((8, 128), weight_ref[lat], F32) / cells
    for p in range(blocks):
        wave = jnp.broadcast_to(waves_f[p : p + 1, :], (8, 128))
        alive = jnp.broadcast_to(waves[p : p + 1, :], (8, 128)) < live
        angles = []
        for steps in (steps_low, steps_high):
            phase = wave * steps
            rest = phase - jnp.round(phase * inverse) * cells
            angles.append(turn(rest * inverse))
        (cos_b, sin_b), (cos_h, sin_h) = angles
        cos8 = jnp.broadcast_to(cos_h[0:1, :], (8, 128))
        sin8 = jnp.broadcast_to(sin_h[0:1, :], (8, 128))
        lo, hi = p * 128, half + p * 128
        held = []
        for b in range(16):
            held.append((cos_b, sin_b))
            if b % 2:
                at = (b - 1) * 8
                table[i, at : at + 16, lo : lo + 128] = jnp.concatenate(
                    [held[b - 1][0], cos_b], 0
                ).astype(BF16)
                table[i, at : at + 16, hi : hi + 128] = jnp.concatenate(
                    [held[b - 1][1], sin_b], 0
                ).astype(BF16)
            if b < 15:
                cos_b, sin_b = cos_b * cos8 - sin_b * sin8, sin_b * cos8 + cos_b * sin8
        scale = jnp.where(alive, jnp.where(wave == 0.0, 1.0, 2.0), 0.0)
        lines = (
            cos_h[1:2, :], sin_h[1:2, :], cos_h[2:3, :], sin_h[2:3, :],
            scale[0:1, :], jnp.where(alive, gain, 0.0)[0:1, :], cells[0:1, :],
        )
        at = (i * blocks + p) * 8
        for n, line in enumerate(lines):
            rotors[at + n : at + n + 1, :] = line


def fill_position(position, where_from, lat_here):
    rows = jnp.concatenate(
        [where_from[i : i + 1, h * 128 : (h + 1) * 128] for i in range(lat_here) for h in range(2)],
        1,
    )
    count = rows.shape[1]
    number = iota((16, count), 1)
    high = jnp.broadcast_to(rows >> 7, (16, count)) == iota((16, count), 0)
    parts = [
        jnp.where(high, part.astype(F32), 0.0).astype(BF16) for part in (number >> 4, number & 15)
    ]
    low = jnp.broadcast_to(rows & 127, (128, count)) == iota((128, count), 0)
    found = lax.dot_general(
        jnp.concatenate(parts, 0),
        jnp.where(low, 1.0, 0.0).astype(BF16),
        NT,
        preferred_element_type=F32,
    )
    position[...] = (found[:16, :] * 16.0 + found[16:, :]).astype(I32)


def turn_pair(turned, leg, p):
    for at in range(0, leg.shape[1] - 1, 128):
        turned[p, :, at : at + 128] = leg[p, at : at + 128, :].T


def inverse_kernel(
    wave_hbm, wave_rows_hbm, spec_hbm, lat_hbm, lat_rows_hbm, active_hbm, weight_hbm, leg_hbm,
    out_ref, leg, last_rows, table, rotors, position, owners,
    wave_ref, wave_rows_ref, spec_ref, lat_ref, lat_rows_ref, active_ref, weight_ref,
    stack, small_sems, sems,
):
    pairs, coef, lat_total = leg_hbm.shape
    lat_here = lat_total // 256
    small = start_copies(
        (
            (lat_rows_hbm, lat_rows_ref),
            (wave_rows_hbm, wave_rows_ref),
            (wave_hbm, wave_ref),
            (spec_hbm, spec_ref),
            (lat_hbm, lat_ref),
            (active_hbm, active_ref),
            (weight_hbm, weight_ref),
        ),
        small_sems,
    )
    copies = start_copies([(leg_hbm.at[p], leg.at[p]) for p in range(pairs)], sems)
    stack[120:128, :] = jnp.zeros((8, 256), F32)
    owners[...] = jnp.zeros_like(owners)
    last_rows[...] = jnp.zeros_like(last_rows)
    for copy in small:
        copy.wait()
    where_from = latitude_table(lat_rows_ref, lat_here)
    fill_position(position, where_from, lat_here)
    waves = wave_table(wave_rows_ref, wave_rows_ref.shape[0])
    wide = lax.axis_index("wide")
    column = iota((2, coef), 1)
    lefts = []
    for p in range(pairs):
        own = column < coef - 1 - wave_ref[wide * 2 * pairs + 2 * p]
        owners[p : p + 1, :coef] = jnp.where(own[:1], 1.0, 0.0)
        rows = spec_ref[p].astype(F32)
        nothing = jnp.zeros_like(rows)
        used = [jnp.where(own, rows, nothing), jnp.where(own, nothing, rows)]
        idle = [nothing, nothing]
        lefts.append(jnp.concatenate(idle + used if p % 2 else used + idle, 0).astype(BF16))
    total = None
    for p in range(pairs):
        for i in range(3 * p, min(3 * p + 3, lat_here)):
            fill_tables(table, rotors, waves, i, lat_ref, active_ref, weight_ref)
        copies[p].wait()
        result = jnp.dot(lefts[p][:, : coef - 1], leg[p, : coef - 1, :], preferred_element_type=F32)
        last = leg[p, coef - 1 : coef, :].astype(F32)
        last_rows[p : p + 1, :] = last
        result = result + lefts[p][:, coef - 1 :].astype(F32) * last
        total = total + result if p % 2 else result
        if p % 2 == 0 and p < pairs - 1:
            continue
        total = total.astype(BF16).astype(F32)
        tiles = [total[:, k * 128 : (k + 1) * 128] for k in range(lat_total // 128)]
        for i in range(lat_here):
            at = i * 24 + p // 2 * 8
            for h in range(2):
                index = jnp.broadcast_to(where_from[i : i + 1, h * 128 : (h + 1) * 128], (8, 128))
                stack[at : at + 8, h * 128 : (h + 1) * 128] = gather_tiles(tiles, index)
    out_ref[...] = stack[...].T


def direct_kernel(recv_ref, position, owners, last_rows, turned, leg, out_ref):
    pairs, _, _, coef = out_ref.shape
    lat_total = turned.shape[1]
    lat_here = lat_total // 256
    rows = recv_ref[...].T
    for group in reversed(range((pairs + 1) // 2)):
        tiles = []
        for i in range(lat_here):
            at = i * 24 + group * 8
            tiles += [rows[at : at + 8, :128], rows[at : at + 8, 128:]]
        ordered = []
        for block in range(lat_total // 128):
            index = jnp.broadcast_to(position[block : block + 1, :], (8, 128))
            ordered.append(gather_tiles(tiles, index))
        left = jnp.concatenate(ordered, 1).astype(BF16)
        for p in group_pairs(group, pairs):
            own = owners[p : p + 1, :coef] > 0.0
            if p < turned.shape[0]:
                result = jnp.dot(left, turned[p], preferred_element_type=F32)
            else:
                block = leg[p, : coef - 1, :]
                result = lax.dot_general(left, block, NT, preferred_element_type=F32)
            last = jnp.sum(left.astype(F32) * last_rows[p : p + 1, :], axis=1, keepdims=True)
            result = jnp.concatenate([result, jnp.broadcast_to(last, (8, 128))], 1)
            at = 4 * (p % 2)
            for r in range(2):
                out_ref[p, r, :, :] = jnp.where(
                    own,
                    result[at + r : at + r + 1, :coef],
                    result[at + 2 + r : at + 3 + r, :coef],
                )


def fourier_kernel(
    recv_ref, table, rotors, wind_ref, leg, grid_hbm, out_ref, turned,
    flat, four, left, backs, grid_ref, sems,
):
    lat_here, levels, points = wind_ref.shape
    half = table.shape[2] // 2
    blocks = half // 128
    outer = points // 128
    for h in range(2):
        flat[h * 128 : (h + 1) * 128, :] = recv_ref[h * 128 : (h + 1) * 128, :].T
    low = iota((32, 128), 1) < 64
    for h in range(2):
        for r in range(2):
            even, odd = (flat[pl.ds(h * 128 + 2 * s + r, 32, stride=4), :] for s in range(2))
            levels_here = (
                jnp.where(low, even, pltpu.roll(odd, 64, 1)),
                jnp.where(low, pltpu.roll(even, 64, 1), odd),
            )
            for n, rows in enumerate(levels_here):
                for copy in range(2):
                    four[pl.ds(r * 256 + copy * 4 + 2 * h + n, 32, stride=8), :] = rows
    backs[...] = jnp.zeros_like(backs)
    upper = iota((8, 128), 0) < 4
    outer_row = iota((outer * 4, 128), 0) >> 2
    point = (outer_row * 128 + iota((outer * 4, 128), 1)).astype(F32)

    def rotor(i, p, n):
        at = (i * blocks + p) * 8 + n
        return jnp.broadcast_to(rotors[at : at + 1, :], (8, 128))

    copies = []
    fields, sums_of = {}, {}

    def inverse_stage(i):
        for p in range(blocks):
            cosx = jnp.where(upper, 1.0, rotor(i, p, 0))
            sinx = jnp.where(upper, 0.0, rotor(i, p, 1))
            cos2, sin2, scale = (rotor(i, p, n) for n in (2, 3, 4))
            lo, hi = p * 128, half + p * 128
            at = (i * 6 + p) * 8
            real = four[at : at + 8, :] * scale
            at = (32 + i * 6 + p) * 8
            imag = four[at : at + 8, :] * scale
            real, imag = real * cosx - imag * sinx, real * sinx + imag * cosx
            held = []
            for a in range(outer // 2):
                held.append((real, imag))
                if a % 2:
                    at = (a - 1) * 8
                    left[i, at : at + 16, lo : lo + 128] = jnp.concatenate(
                        [held[a - 1][0], real], 0
                    ).astype(BF16)
                    left[i, at : at + 16, hi : hi + 128] = -jnp.concatenate(
                        [held[a - 1][1], imag], 0
                    ).astype(BF16)
                if a < outer // 2 - 1:
                    real, imag = real * cos2 - imag * sin2, real * sin2 + imag * cos2
        if i < turned.shape[0]:
            turn_pair(turned, leg, i)
        values = lax.dot_general(left[i], table[i], NT, preferred_element_type=F32)
        cells = jnp.broadcast_to(rotors[i * blocks * 8 + 6 : i * blocks * 8 + 7, :], point.shape)
        values = jnp.where(point < cells, values, 0.0).astype(BF16).astype(F32)
        fields[i] = values

    def product_stage(i):
        values = fields[i]
        winds = [
            wind_ref[i, :, a * 128 : (a + 1) * 128].astype(F32) for a in range(outer)
        ]
        product = (values * jnp.concatenate(winds, 0)).astype(BF16)
        sums_of[i] = jnp.dot(product, table[i], preferred_element_type=F32)

    def direct_stage(i):
        sums = sums_of[i]
        values = fields[i]
        for a in range(outer):
            grid_ref[i, :, a * 128 : (a + 1) * 128] = values[a * 4 : a * 4 + 4, :].astype(BF16)
        copies.extend(start_copies([(grid_ref.at[i], grid_hbm.at[i])], sems.at[pl.ds(i, 1)]))
        for p in range(blocks):
            cosx = jnp.where(upper, 1.0, rotor(i, p, 0))
            sinx = jnp.where(upper, 0.0, rotor(i, p, 1))
            cos2, sin2, gain = (rotor(i, p, n) for n in (2, 3, 5))
            lo, hi = p * 128, half + p * 128
            last = outer * 4 - 8
            real = sums[last : last + 8, lo : lo + 128]
            imag = sums[last : last + 8, hi : hi + 128]
            for at in range(last - 8, -1, -8):
                real, imag = (
                    sums[at : at + 8, lo : lo + 128] + (real * cos2 - imag * sin2),
                    sums[at : at + 8, hi : hi + 128] + (real * sin2 + imag * cos2),
                )
            real, imag = real * cosx - imag * sinx, real * sinx + imag * cosx
            real = real + pltpu.roll(real, 4, 0)
            imag = imag + pltpu.roll(imag, 4, 0)
            both = jnp.where(upper, real, -imag) * gain
            at = (i * 6 + p) * 4
            backs[at : at + 4, :] = both[0:4, :]
            at = (32 + i * 6 + p) * 4
            backs[at : at + 4, :] = both[4:8, :]

    for step in range(lat_here + 2):
        if step < lat_here:
            inverse_stage(step)
        if 1 <= step <= lat_here:
            product_stage(step - 1)
        if step >= 2:
            direct_stage(step - 2)

    for h in range(2):
        for r in range(2):
            even, odd = (backs[pl.ds(r * 128 + 2 * h + n, 32, stride=4), :] for n in range(2))
            slots = (
                jnp.where(low, even, pltpu.roll(odd, 64, 1)),
                jnp.where(low, pltpu.roll(even, 64, 1), odd),
            )
            for s, rows in enumerate(slots):
                flat[pl.ds(h * 128 + 2 * s + r, 32, stride=4), :] = rows
    for h in range(2):
        out_ref[h * 128 : (h + 1) * 128, :] = flat[h * 128 : (h + 1) * 128, :].T
    for copy in copies:
        copy.wait()


def vmem():
    return pl.BlockSpec(memory_space=pltpu.VMEM)


def hbm():
    return pl.BlockSpec(memory_space=pltpu.HBM)


def in_hbm(x):
    return pltpu.with_memory_space_constraint(x, pltpu.HBM)


def exchange(rows):
    count, width = rows.shape
    moved = lax.all_to_all(
        rows.reshape(count, 1, width), ("lev", "wide"), split_axis=0, concat_axis=0, tiled=True
    )
    return moved.reshape(count, width)


def shards(spec_in, legendre, wind, lat_weight, wave_order, lat_order, active):
    pairs, coef, lat_total = legendre.shape
    lat_here, levels, points = wind.shape
    devices = lat_total // lat_here
    limit = pltpu.CompilerParams(vmem_limit_bytes=24 * 1024 * 1024)
    lat_rows = lat_order.reshape(lat_total // 128, 128)
    wave_rows = wave_order.reshape(wave_order.shape[0] // 128, 128)

    waves = wave_order.shape[0]
    wide_coef = (coef + 127) // 128 * 128
    operands = (
        wave_order, wave_rows, spec_in.reshape(pairs, 2, coef), lat_order, lat_rows, active,
        lat_weight, legendre,
    )
    outgoing, leg_here, last_rows, table, rotors, position, owners = pl.pallas_call(
        inverse_kernel,
        name="legendre_inverse",
        out_shape=(
            jax.ShapeDtypeStruct((devices, 128), F32),
            jax.ShapeDtypeStruct(legendre.shape, BF16),
            jax.ShapeDtypeStruct((8, lat_total), F32),
            jax.ShapeDtypeStruct((lat_here, 128, 2 * waves), BF16),
            jax.ShapeDtypeStruct((lat_here * waves // 128 * 8, 128), F32),
            jax.ShapeDtypeStruct((16, 128), I32),
            jax.ShapeDtypeStruct((8, wide_coef), F32),
        ),
        in_specs=[hbm()] * len(operands),
        out_specs=(vmem(),) * 7,
        scratch_shapes=[
            pltpu.SMEM(wave_order.shape, I32),
            pltpu.VMEM(wave_rows.shape, I32),
            pltpu.VMEM((pairs, 2, coef), BF16),
            pltpu.SMEM(lat_order.shape, I32),
            pltpu.VMEM(lat_rows.shape, I32),
            pltpu.SMEM(active.shape, I32),
            pltpu.SMEM(lat_weight.shape, F32),
            pltpu.VMEM((128, devices), F32),
            pltpu.SemaphoreType.DMA((7,)),
            pltpu.SemaphoreType.DMA((pairs,)),
        ],
        compiler_params=limit,
    )(*(in_hbm(x) for x in operands))
    arrived = exchange(outgoing)

    grid, outgoing, turned = pl.pallas_call(
        fourier_kernel,
        name="fourier",
        out_shape=(
            jax.ShapeDtypeStruct(wind.shape, BF16),
            jax.ShapeDtypeStruct((devices, 128), F32),
            jax.ShapeDtypeStruct((3, lat_total, coef - 1), BF16),
        ),
        in_specs=[vmem()] * 5,
        out_specs=(hbm(), vmem(), vmem()),
        scratch_shapes=[
            pltpu.VMEM((devices, 128), F32),
            pltpu.VMEM((512, 128), F32),
            pltpu.VMEM((lat_here, points // 32, 2 * waves), BF16),
            pltpu.VMEM((256, 128), F32),
            pltpu.VMEM(wind.shape, BF16),
            pltpu.SemaphoreType.DMA((lat_here,)),
        ],
        compiler_params=limit,
    )(arrived, table, rotors, wind, leg_here)

    arrived = exchange(outgoing)
    spec_out = pl.pallas_call(
        direct_kernel,
        name="legendre_direct",
        out_shape=jax.ShapeDtypeStruct((pairs, 2, 1, coef), F32),
        in_specs=[vmem()] * 6,
        out_specs=vmem(),
        compiler_params=limit,
    )(arrived, position, owners, last_rows, turned, leg_here)
    return (grid, spec_out)


def solution(mesh):
    in_specs = (
        P("wide", None, "lev", None),
        P("wide", None, None),
        P(("wide", "lev"), None, None),
        P(),
        P(),
        P(),
        P(),
    )
    out_specs = (P(("wide", "lev"), None, None), P("wide", None, "lev", None))
    return jax.shard_map(shards, mesh=mesh, in_specs=in_specs, out_specs=out_specs, check_vma=False)
```
